32 devices in a mesh: grp: 4 (over x, core), seq: 8 (over z, y).
Axes of the slice: x: 2, y: 2, z: 4, core: 2. Of those that a mesh axis runs over, the one named last changes fastest.
Arguments:
- targets: bfloat16 [16384, 1024], P(('grp', 'seq')), may hold values from -30 to 30
- context: bfloat16 [256, 1024], P('seq'), may hold values from -9 to 9
- w_query: bfloat16 [1024, 1024], replicated, as said below
- w_key: bfloat16 [1024, 1024], replicated, as said below
- w_value: bfloat16 [1024, 1024], replicated, may hold values from -0.1875 to 0.1875
- w_out: bfloat16 [1024, 1024], replicated, may hold values from -0.1875 to 0.1875
- visible: int32 [8, 16], replicated, may hold values from 0 to 1, as said below
- grad_out: bfloat16 [16384, 1024], P(('grp', 'seq')), may hold values from -24 to 24
Outputs:
- d_targets: bfloat16 [16384, 1024], P(('grp', 'seq'))
- d_context: bfloat16 [256, 1024], P(('grp', 'seq'))
- grad_wq: float32 [1024, 1024], P(('grp', 'seq'))
- grad_wo: float32 [1024, 1024], P(('grp', 'seq'))
The draws below stay inside these ranges and needn't reach their ends.
Inputs may be any that keep to these rules, and one draw needn't show every extreme that they name: Every row of visible holds at least one 1. `w_query`: entries have a spread of about one over the square root of 1024. `w_key`: entries have a spread of about one over the square root of 1024.
All inputs are finite; a program needn't handle non-finite values.
Results may differ from the reference program's by a relative error of at most 0.018.
The reference program's roundings to bfloat16 on the way (of `grad_attn`, `probs`, `attended`, `grad_logits` and `query_grad`) count: a program that leaves them out, or rounds other values in their place, can miss the bound.
Values may be sent and summed in bfloat16 or wider, within the bound.
No kernel may reach another device: no remote copies, remote signals or barrier semaphores. Data moves between devices by JAX's collectives and lax.ppermute only.
A program may use at most 128 MiB of HBM per device.

```python
import math
import jax
import jax.numpy as jnp
from jax import lax

D = 1024
HEADS = 16
DH = 64
TVIEWS = 8
CVIEWS = 16
TGT = 16384
CTX = 256


def chosen_views(key):
    offsets = jax.random.randint(jax.random.fold_in(key, 7), (TVIEWS, 1), 0, CVIEWS, dtype=jnp.int32)
    return (jnp.arange(TVIEWS, dtype=jnp.int32)[:, None] * 2 + offsets) % CVIEWS


def draw_visible(key, part):
    coins = jax.random.randint(key, (TVIEWS, CVIEWS), 0, 2, dtype=jnp.int32)
    chosen = chosen_views(key)
    forced = (jnp.arange(CVIEWS, dtype=jnp.int32)[None, :] == chosen).astype(jnp.int32)
    return jnp.maximum(coins, forced)


def directions(key):
    return jax.random.uniform(jax.random.fold_in(key, 11), (CVIEWS, D), jnp.float32, -1.75, 1.75)


def drawn_rows(key, count):
    return jnp.clip(1.5 * jax.random.normal(key, (count, D), jnp.float32), -9.0, 9.0)


def draw_context(key, part):
    view_rows = CTX // CVIEWS
    base = drawn_rows(jax.random.fold_in(key, 31), CTX)
    towards = directions(key)
    noise = jax.random.uniform(jax.random.fold_in(key, 12), (CVIEWS, D), jnp.float32, -1.75, 1.75)
    spots = jax.random.randint(jax.random.fold_in(key, 13), (CVIEWS,), 0, view_rows - 1, dtype=jnp.int32)
    spots = spots + jnp.arange(CVIEWS, dtype=jnp.int32) * view_rows
    base = base.at[spots].set(2.5 * towards)
    base = base.at[spots + 1].set(2.5 * (0.985 * towards + 0.05 * noise))
    return base.astype(jnp.bfloat16)


def draw_targets(key, part):
    view_rows = TGT // TVIEWS
    quarter = view_rows // 4
    base = drawn_rows(jax.random.fold_in(key, 41), TGT)
    towards = directions(key)
    views = chosen_views(key)[:, 0]
    jitter = jax.random.randint(jax.random.fold_in(key, 42), (TVIEWS, 4), 0, quarter, dtype=jnp.int32)
    places = jnp.arange(TVIEWS, dtype=jnp.int32)[:, None] * view_rows + jnp.arange(4, dtype=jnp.int32)[None, :] * quarter + jitter
    strengths = jnp.array([8.0, 11.0, 14.0, 17.0], jnp.float32)
    aligned = strengths[None, :, None] * towards[views][:, None, :]
    base = base.at[places.reshape(TVIEWS * 4)].set(aligned.reshape(TVIEWS * 4, D))
    return base.astype(jnp.bfloat16)


def weight_pair(key):
    first = jnp.clip(jax.random.normal(jax.random.fold_in(key, 61), (D, D), jnp.float32), -6.0, 6.0) * D ** (-0.5)
    second = jnp.clip(jax.random.normal(jax.random.fold_in(key, 62), (D, D), jnp.float32), -6.0, 6.0) * D ** (-0.5)
    return (first, 0.8 * first + 0.6 * second)


def draw_w_query(key, part):
    return weight_pair(key)[0].astype(jnp.bfloat16)


def draw_w_key(key, part):
    return weight_pair(key)[1].astype(jnp.bfloat16)


def levels(key, extent, pieces, least, largest):
    factor_of = 1.0
    for axis_at, shards_of in pieces:
        heights = jax.random.uniform(jax.random.fold_in(jax.random.fold_in(key, 6), axis_at), (shards_of,), jnp.float32, least / len(pieces), largest / len(pieces))
        factor_of = factor_of * jnp.repeat(jnp.exp(heights), extent[axis_at] // shards_of).reshape((-1,) + (1,) * (len(extent) - 1 - axis_at))
    return factor_of


def bell_draw(own_key, extent, scale, most, cuts=(), held_as=jnp.bfloat16):
    values = scale * jax.random.normal(own_key, extent, jnp.float32)
    if cuts:
        values = values * levels(own_key, extent, cuts, -0.22, 0.18)
    return jnp.clip(values, -most, most).astype(held_as)


def setup_inputs(seed: int = 0) -> dict:
    splits = jax.random.split(jax.random.key(seed), 9)
    return {
        "targets": draw_targets(jax.random.fold_in(splits[8], 71), 0),
        "context": draw_context(jax.random.fold_in(splits[8], 71), 0),
        "w_query": draw_w_query(jax.random.fold_in(splits[8], 71), 0),
        "w_key": draw_w_key(jax.random.fold_in(splits[8], 71), 0),
        "w_value": bell_draw(splits[4], (D, D), D ** -0.5, 0.1875),
        "w_out": bell_draw(splits[5], (D, D), D ** -0.5, 0.1875),
        "visible": draw_visible(jax.random.fold_in(splits[8], 71), 0),
        "grad_out": bell_draw(splits[7], (TGT, D), 4.0, 24.0, ((0, 32),)),
    }


def head_split(matrix):
    return matrix.astype(jnp.float32).reshape(matrix.shape[0], HEADS, DH)


def reference(targets, context, w_query, w_key, w_value, w_out, visible, grad_out):
    queries = jnp.dot(targets, w_query, preferred_element_type=jnp.float32).astype(jnp.bfloat16)
    keys_all = jnp.dot(context, w_key, preferred_element_type=jnp.float32).astype(jnp.bfloat16)
    values_all = jnp.dot(context, w_value, preferred_element_type=jnp.float32).astype(jnp.bfloat16)
    grad_attn = jnp.dot(grad_out, w_out.T, preferred_element_type=jnp.float32).astype(jnp.bfloat16)
    score_scale = DH ** -0.5
    key_heads = head_split(keys_all)
    value_heads = head_split(values_all)
    key_views = jnp.arange(CTX, dtype=jnp.int32) // (CTX // CVIEWS)
    block_rows = math.gcd(TGT, 512)
    blocks = TGT // block_rows

    def one_block(totals, inputs):
        key_grad, value_grad = totals
        query_blk, grad_blk, first_row = inputs
        query_views = (first_row + jnp.arange(block_rows, dtype=jnp.int32)) // (TGT // TVIEWS)
        allowed = (visible[query_views][:, key_views] == 1)[None]
        query_heads = head_split(query_blk)
        grad_heads = head_split(grad_blk)
        scores = jnp.einsum("bhd,khd->hbk", query_heads, key_heads) * score_scale
        masked = jnp.where(allowed, scores, -1e30)
        row_max = jnp.max(masked, axis=2, keepdims=True)
        unnormed = jnp.where(allowed, jnp.exp(masked - row_max), 0.0)
        row_sum = jnp.sum(unnormed, axis=2, keepdims=True)
        probs_low = lax.optimization_barrier((unnormed / row_sum).astype(jnp.bfloat16))
        probs = probs_low.astype(jnp.float32)
        attended = jnp.einsum("hbk,khd->bhd", probs, value_heads).reshape(block_rows, D).astype(jnp.bfloat16)
        row_dot = jnp.sum(head_split(attended) * grad_heads, axis=2).T[:, :, None]
        grad_scores = jnp.einsum("bhd,khd->hbk", grad_heads, value_heads)
        logits_low = lax.optimization_barrier((probs * (grad_scores - row_dot)).astype(jnp.bfloat16))
        grad_logits = logits_low.astype(jnp.float32)
        query_grad = (jnp.einsum("hbk,khd->bhd", grad_logits, key_heads) * score_scale).reshape(block_rows, D).astype(jnp.bfloat16)
        key_grad = key_grad + (jnp.einsum("hbk,bhd->khd", grad_logits, query_heads) * score_scale).reshape(CTX, D)
        value_grad = value_grad + jnp.einsum("hbk,bhd->khd", probs, grad_heads).reshape(CTX, D)
        return (key_grad, value_grad), (attended, query_grad)

    inputs = (queries.reshape(blocks, block_rows, D), grad_attn.reshape(blocks, block_rows, D),
              jnp.arange(blocks, dtype=jnp.int32) * block_rows)
    empty_grad = jnp.zeros((CTX, D), jnp.float32)
    (key_grad, value_grad), (attended, query_grad) = lax.scan(one_block, (empty_grad, empty_grad), inputs)
    attended = attended.reshape(TGT, D)
    query_grad = query_grad.reshape(TGT, D)
    weight_stack = jnp.concatenate([w_key.T, w_value.T], axis=0).astype(jnp.float32)
    both_grads = jnp.concatenate([key_grad, value_grad], axis=1)
    d_context = jnp.dot(both_grads, weight_stack, precision=lax.Precision.HIGHEST).astype(jnp.bfloat16)
    d_targets = jnp.dot(query_grad, w_query.T, preferred_element_type=jnp.float32).astype(jnp.bfloat16)
    grad_wq = jnp.dot(targets.T, query_grad, preferred_element_type=jnp.float32)
    grad_wo = jnp.dot(attended.T, grad_out, preferred_element_type=jnp.float32)
    return (d_targets, d_context, grad_wq, grad_wo)
```

```python
from functools import partial

import jax
import jax.numpy as jnp
from jax import lax
from jax.experimental import pallas as pl
from jax.experimental.pallas import tpu as pltpu
from jax.sharding import PartitionSpec as P

HEADS = 16
TVIEWS = 8
CVIEWS = 16
AXES = ("grp", "seq")
CHUNK = 256

F32 = jnp.float32
BF16 = jnp.bfloat16


def dot(left, right, dims):
    return lax.dot_general(left, right, (dims, ((), ())), preferred_element_type=F32)


def forward_kernel(chunk, block_rows, q_ref, k_ref, v_ref, bias_ref, att_ref, probs_ref):
    rows = q_ref.shape[1]
    key_block = k_ref[...]
    value_block = v_ref[...]
    for start in range(0, rows, chunk):
        cols = pl.ds(start, chunk)
        scores = dot(key_block, q_ref[:, cols], ((0,), (0,)))
        scores = scores + bias_ref[start // block_rows][:, :1]
        row_max = jnp.max(scores, axis=0, keepdims=True)
        unnormed = jnp.exp(scores - row_max)
        row_sum = jnp.sum(unnormed, axis=0, keepdims=True)
        probs = (unnormed * (1.0 / row_sum)).astype(BF16)
        probs_ref[0, :, cols] = probs
        att_ref[:, cols] = dot(value_block, probs, ((1,), (0,))).astype(BF16)


def backward_kernel(
    chunk, scale, q_ref, g_ref, k_ref, v_ref, att_ref, probs_ref, qg_ref, kvg_ref
):
    rows = q_ref.shape[1]
    key_block = k_ref[...]
    value_block = v_ref[...]
    key_grad = jnp.zeros(key_block.shape, F32)
    value_grad = jnp.zeros(key_block.shape, F32)
    for start in range(0, rows, chunk):
        cols = pl.ds(start, chunk)
        grad = g_ref[:, cols]
        probs = probs_ref[0, :, cols]
        row_dot = jnp.sum(att_ref[:, cols].astype(F32) * grad.astype(F32), axis=0, keepdims=True)
        grad_scores = dot(value_block, grad, ((0,), (0,)))
        logits = (probs.astype(F32) * (grad_scores - row_dot)).astype(BF16)
        qg_ref[:, cols] = dot(key_block, logits, ((1,), (0,))).astype(BF16)
        key_grad += dot(q_ref[:, cols], logits, ((1,), (1,)))
        value_grad += dot(grad, probs, ((1,), (1,)))
    kvg_ref[0] = (key_grad * scale).astype(BF16)
    kvg_ref[1] = value_grad.astype(BF16)


def on_device(targets, context, w_query, w_key, w_value, w_out, visible, grad_out):
    query_rows, width = targets.shape
    head_size = width // HEADS
    score_scale = head_size ** (-0.5)
    grp_count = lax.axis_size("grp")
    seq_count = lax.axis_size("seq")
    device_count = grp_count * seq_count
    grp = lax.axis_index("grp")
    seq = lax.axis_index("seq")
    me = grp * seq_count + seq
    core = grp % 2
    core_mask = seq_count
    high_count = grp_count // 2
    half_width = width // 2
    half_heads = HEADS // 2
    context_rows = context.shape[0] * seq_count

    def swap(array, mask):
        return lax.ppermute(array, AXES, [(i, i ^ mask) for i in range(device_count)])

    def bit_of(mask):
        return (me // mask) % 2

    own_half = context.shape[0] // 2
    held = lax.dynamic_slice_in_dim(context, core * own_half, own_half, 0)[None]
    mask = 1
    while mask < seq_count:
        other = swap(held, mask)
        upper = bit_of(mask) == 1
        held = jnp.concatenate(
            [jnp.where(upper, other, held), jnp.where(upper, held, other)], axis=0
        )
        mask *= 2
    other = swap(held, core_mask)
    held = jnp.stack(
        [jnp.where(core == 1, other, held), jnp.where(core == 1, held, other)], axis=1
    )
    context_all = held.reshape(context_rows, width)

    targets_two = jnp.concatenate([targets, swap(targets, core_mask)], axis=0)
    grad_two = jnp.concatenate([grad_out, swap(grad_out, core_mask)], axis=0)

    def columns_of(matrix, which):
        split = matrix.reshape(width, high_count, 2, width // grp_count)
        return lax.dynamic_index_in_dim(split, which, 2, keepdims=False).reshape(width, half_width)

    wq_mine = columns_of(w_query, core)
    wq_both = jnp.concatenate([wq_mine, columns_of(w_query, 1 - core)], axis=1)
    wkv = jnp.concatenate([columns_of(w_key, core), columns_of(w_value, core)], axis=1)
    wo_mine = lax.dynamic_index_in_dim(
        w_out.reshape(high_count, 2, width // grp_count, width), core, 1, keepdims=False
    ).reshape(half_width, width)

    queries = dot(wq_mine, targets_two, ((0,), (1,))).astype(BF16)
    grads = dot(wo_mine, grad_two, ((1,), (1,))).astype(BF16)
    kv_scale = jnp.where(jnp.arange(width) < half_width, score_scale, 1.0).astype(BF16)
    key_values = dot(wkv, context_all, ((0,), (1,))).astype(BF16) * kv_scale[:, None]

    view_rows = query_rows * device_count // TVIEWS
    context_view = context_rows // CVIEWS
    firsts = jnp.stack([me, me ^ core_mask]) * query_rows
    seen = visible[firsts // view_rows]
    seen = jnp.repeat(seen, context_view, axis=1)
    bias = jnp.where(seen == 1, 0.0, -1e30).astype(F32)
    bias = jnp.broadcast_to(bias[:, :, None], (2, context_rows, 128))

    rows = 2 * query_rows
    head_rows = pl.BlockSpec((head_size, rows), lambda h: (h, 0))
    key_spec = pl.BlockSpec((head_size, context_rows), lambda h: (h, 0))
    value_spec = pl.BlockSpec((head_size, context_rows), lambda h: (h + half_heads, 0))
    probs_spec = pl.BlockSpec((1, context_rows, rows), lambda h: (h, 0, 0))
    wide = jax.ShapeDtypeStruct((half_width, rows), BF16)
    unit = 2 * half_width * rows * context_rows

    attended, probs = pl.pallas_call(
        partial(forward_kernel, CHUNK, query_rows),
        grid=(half_heads,),
        in_specs=[
            head_rows,
            key_spec,
            value_spec,
            pl.BlockSpec((2, context_rows, 128), lambda h: (0, 0, 0)),
        ],
        out_specs=[head_rows, probs_spec],
        out_shape=[wide, jax.ShapeDtypeStruct((half_heads, context_rows, rows), BF16)],
        cost_estimate=pl.CostEstimate(
            flops=8 * unit, bytes_accessed=8 << 20, transcendentals=unit // 128
        ),
        name="attend",
    )(queries, key_values, key_values, bias)

    wo_term = dot(attended, grad_two, ((1,), (0,))).astype(BF16)

    query_grad, kv_grad = pl.pallas_call(
        partial(backward_kernel, CHUNK, score_scale),
        grid=(half_heads,),
        in_specs=[head_rows, head_rows, key_spec, value_spec, head_rows, probs_spec],
        out_specs=[
            head_rows,
            pl.BlockSpec((2, head_size, context_rows), lambda h: (0, h, 0)),
        ],
        out_shape=[wide, jax.ShapeDtypeStruct((2, half_width, context_rows), BF16)],
        cost_estimate=pl.CostEstimate(flops=8 * unit, bytes_accessed=8 << 20, transcendentals=0),
        name="attend_back",
    )(queries, grads, key_values, key_values, attended, probs)

    wq_term = dot(targets_two, query_grad, ((0,), (1,))).astype(BF16)
    ctx_term = dot(kv_grad.reshape(width, context_rows), wkv, ((0,), (1,))).astype(BF16)

    high_masks = []
    mask = core_mask * high_count
    while mask > core_mask:
        high_masks.append(mask)
        mask //= 2
    seq_masks = []
    mask = seq_count // 2
    while mask >= 1:
        seq_masks.append(mask)
        mask //= 2
    all_masks = high_masks + seq_masks
    bits = [2] * len(all_masks)
    first, second = high_masks[-1], seq_masks[-1]
    rest = seq_masks[-2::-1] + high_masks[:-1]

    def halve(array, masks, mask, last=False):
        axis = masks.index(mask)
        bit = bit_of(mask)
        sent = lax.dynamic_index_in_dim(array, 1 - bit, axis, keepdims=False)
        kept = lax.dynamic_index_in_dim(array, bit, axis, keepdims=False)
        total = kept.astype(F32) + swap(sent, mask).astype(F32)
        left = masks[:axis] + masks[axis + 1 :]
        return (total if last else total.astype(BF16)), left

    def reduce_scatter(array):
        cut = array.shape[-1] // 2
        one, masks_one = halve(array[..., :cut], all_masks, first)
        two, masks_two = halve(array[..., cut:], all_masks, second)
        one, masks = halve(one, masks_one, second)
        two, _ = halve(two, masks_two, first)
        both = jnp.concatenate([one, two], axis=-1)
        for step, mask in enumerate(rest):
            both, masks = halve(both, masks, mask, step == len(rest) - 1)
        return both

    out_rows = width // device_count
    ctx_out = context_rows // device_count
    grad_wo = reduce_scatter(wo_term.reshape(*bits, out_rows, width))

    ctx_split = ctx_term.reshape(high_count, 2, seq_count, ctx_out, width)
    ctx_kept = lax.dynamic_index_in_dim(ctx_split, core, 1, keepdims=False)
    ctx_sent = lax.dynamic_index_in_dim(ctx_split, 1 - core, 1, keepdims=False)
    ctx_pair = (ctx_kept.astype(F32) + swap(ctx_sent, core_mask).astype(F32)).astype(BF16)
    ctx_part = jnp.swapaxes(
        ctx_pair.reshape(high_count * seq_count, ctx_out, 2, half_width), 1, 2
    ).reshape(high_count * seq_count, 2 * ctx_out, half_width)
    wq_part = jnp.swapaxes(
        wq_term.reshape(high_count, 2, seq_count, out_rows, half_width), 1, 2
    ).reshape(high_count * seq_count, 2 * out_rows, half_width)
    tail = jnp.concatenate([wq_part, ctx_part], axis=1)
    tail = reduce_scatter(tail.reshape(*bits, 2 * out_rows + 2 * ctx_out, half_width))

    wq_sum = tail[: 2 * out_rows].reshape(2, out_rows, half_width)
    mine = lax.dynamic_index_in_dim(wq_sum, core, 0, keepdims=False)
    theirs = swap(lax.dynamic_index_in_dim(wq_sum, 1 - core, 0, keepdims=False), core_mask)
    mine = mine.reshape(out_rows, high_count, width // grp_count)
    theirs = theirs.reshape(out_rows, high_count, width // grp_count)
    grad_wq = jnp.stack(
        [jnp.where(core == 0, mine, theirs), jnp.where(core == 0, theirs, mine)], axis=2
    ).reshape(out_rows, width)
    ctx_sum = tail[2 * out_rows :].reshape(2, ctx_out, half_width)
    d_context = jnp.swapaxes(ctx_sum, 0, 1).reshape(ctx_out, width).astype(BF16)

    back = swap(query_grad[:, query_rows:], core_mask)
    query_both = jnp.concatenate([query_grad[:, :query_rows], back], axis=0)
    d_targets = dot(query_both, wq_both, ((0,), (1,))).astype(BF16)
    return (d_targets, d_context, grad_wq, grad_wo)


def solution(mesh):
    in_specs = (
        P(AXES, None),
        P("seq", None),
        P(),
        P(),
        P(),
        P(),
        P(),
        P(AXES, None),
    )
    out_specs = (P(AXES, None), P(AXES, None), P(AXES, None), P(AXES, None))
    return jax.shard_map(
        on_device, mesh=mesh, in_specs=in_specs, out_specs=out_specs, check_vma=False
    )
```

```python
from functools import partial

import jax
import jax.numpy as jnp
from jax import lax
from jax.experimental import pallas as pl
from jax.experimental.pallas import tpu as pltpu
from jax.sharding import PartitionSpec as P

HEADS = 16
TVIEWS = 8
CVIEWS = 16
AXES = ("grp", "seq")

F32 = jnp.float32
BF16 = jnp.bfloat16


def dot(left, right, dims):
    return lax.dot_general(left, right, (dims, ((), ())), preferred_element_type=F32)


def query_kernel(core_ref, weight_ref, own_ref, partner_ref, out_ref):
    rows = own_ref.shape[0]
    weight = weight_ref[...]
    out_ref[:, :rows] = dot(own_ref[...], weight, ((1,), (0,))).astype(BF16).T
    out_ref[:, rows:] = dot(partner_ref[...], weight, ((1,), (0,))).astype(BF16).T


def grad_kernel(core_ref, weight_ref, own_ref, partner_ref, out_ref):
    rows = own_ref.shape[0]
    weight = weight_ref[...]
    out_ref[:, :rows] = dot(weight, own_ref[...], ((1,), (1,))).astype(BF16)
    out_ref[:, rows:] = dot(weight, partner_ref[...], ((1,), (1,))).astype(BF16)


def attend_kernel(
    heads,
    scale,
    core_ref,
    context_ref,
    wk_ref,
    wv_ref,
    q_ref,
    own_ref,
    partner_ref,
    bias_ref,
    kv_ref,
    probs_ref,
    att_ref,
    wo_ref,
):
    block_rows = own_ref.shape[0]
    keys = context_ref.shape[0]
    size = q_ref.shape[0] // heads
    context = context_ref[...]
    key_block = (dot(context, wk_ref[...], ((1,), (0,))).astype(BF16).astype(F32) * scale).astype(
        BF16
    )
    value_block = dot(context, wv_ref[...], ((1,), (0,))).astype(BF16)
    kv_ref[0] = key_block.T
    kv_ref[1] = value_block.T
    lane = lax.broadcasted_iota(jnp.int32, (keys, 2 * block_rows), 1)
    bias = jnp.where(lane < block_rows, bias_ref[0][:, :1], bias_ref[1][:, :1])
    for head in range(heads):
        part = pl.ds(head * size, size)
        scores = dot(kv_ref[0, part, :].T, q_ref[part, :], ((1,), (0,))) + bias
        row_max = jnp.max(scores, axis=0, keepdims=True)
        unnormed = jnp.exp(scores - row_max)
        row_sum = jnp.sum(unnormed, axis=0, keepdims=True)
        probs = (unnormed * (1.0 / row_sum)).astype(BF16)
        probs_ref[head] = probs
        att_ref[part, :] = dot(kv_ref[1, part, :], probs, ((1,), (0,))).astype(BF16)
    total = dot(att_ref[:, :block_rows], own_ref[...], ((1,), (0,)))
    total += dot(att_ref[:, block_rows:], partner_ref[...], ((1,), (0,)))
    wo_ref[...] = total.astype(BF16)


def back_kernel(
    heads,
    scale,
    core_ref,
    wk_ref,
    wv_ref,
    q_ref,
    g_ref,
    kv_ref,
    probs_ref,
    att_ref,
    own_ref,
    partner_ref,
    prior_ref,
    qg_own_ref,
    qg_partner_ref,
    wq_ref,
    ctx_ref,
):
    block_rows = own_ref.shape[0]
    size = q_ref.shape[0] // heads
    key_parts, value_parts = [], []
    for head in range(heads):
        part = pl.ds(head * size, size)
        grad = g_ref[part, :]
        probs = probs_ref[head]
        row_dot = jnp.sum(att_ref[part, :].astype(F32) * grad.astype(F32), axis=0, keepdims=True)
        grad_scores = dot(kv_ref[1, part, :].T, grad, ((1,), (0,)))
        value_parts.append(dot(grad, probs, ((1,), (1,))))
        logits = (probs.astype(F32) * (grad_scores - row_dot)).astype(BF16)
        query_grad = dot(kv_ref[0, part, :], logits, ((1,), (0,))).astype(BF16)
        qg_own_ref[part, :] = query_grad[:, :block_rows]
        qg_partner_ref[part, :] = query_grad[:, block_rows:]
        key_parts.append(dot(q_ref[part, :], logits, ((1,), (1,))) * scale)
    weight = dot(qg_own_ref[...], own_ref[...], ((1,), (0,)))
    weight += dot(qg_partner_ref[...], partner_ref[...], ((1,), (0,)))
    wq_ref[...] = weight.astype(BF16).T
    key_grad = jnp.concatenate(key_parts, axis=0).astype(BF16).T
    value_grad = jnp.concatenate(value_parts, axis=0).astype(BF16).T
    term = dot(key_grad, wk_ref[...], ((1,), (1,))) + dot(value_grad, wv_ref[...], ((1,), (1,)))

    @pl.when(pl.program_id(0) == 0)
    def _():
        ctx_ref[...] = prior_ref[...] + term

    @pl.when(pl.program_id(0) > 0)
    def _():
        ctx_ref[...] += term


def targets_kernel(core_ref, mine_ref, theirs_ref, wq_mine_ref, wq_theirs_ref, out_ref, acc_ref):
    term = dot(mine_ref[...], wq_mine_ref[...], ((0,), (1,)))
    term += dot(theirs_ref[...], wq_theirs_ref[...], ((0,), (1,)))
    step = pl.program_id(0)

    @pl.when(step == 0)
    def _():
        acc_ref[...] = term

    @pl.when(step > 0)
    def _():
        acc_ref[...] += term

    @pl.when(step == pl.num_programs(0) - 1)
    def _():
        out_ref[...] = acc_ref[...].astype(BF16)


def fixed(shape):
    return pl.BlockSpec(
        shape, lambda i, core: (0,) * len(shape), pipeline_mode=pl.Buffered(buffer_count=1)
    )


def call(kernel, name, steps, in_specs, out_specs, out_shape, flops, scratch=(), aliases=None):
    return pl.pallas_call(
        kernel,
        grid_spec=pltpu.PrefetchScalarGridSpec(
            num_scalar_prefetch=1,
            grid=(steps,),
            in_specs=in_specs,
            out_specs=out_specs,
            scratch_shapes=scratch,
        ),
        out_shape=out_shape,
        input_output_aliases=aliases or {},
        cost_estimate=pl.CostEstimate(flops=flops, bytes_accessed=4 << 20, transcendentals=0),
        name=name,
    )


def on_device(targets, context, w_query, w_key, w_value, w_out, visible, grad_out):
    query_rows, width = targets.shape
    head_size = width // HEADS
    score_scale = head_size ** (-0.5)
    grp_count = lax.axis_size("grp")
    seq_count = lax.axis_size("seq")
    device_count = grp_count * seq_count
    grp = lax.axis_index("grp")
    seq = lax.axis_index("seq")
    me = grp * seq_count + seq
    core = grp % 2
    core_mask = seq_count
    high_count = grp_count // 2
    half_width = width // 2
    block = width // grp_count
    context_rows = context.shape[0] * seq_count
    rows = 2 * query_rows
    core_index = core.reshape(1).astype(jnp.int32)

    def swap(array, mask):
        return lax.ppermute(array, AXES, [(i, i ^ mask) for i in range(device_count)])

    def bit_of(mask):
        return (me // mask) % 2

    def shaped(*shape, dtype=BF16):
        return jax.ShapeDtypeStruct(shape, dtype)

    own_half = context.shape[0] // 2
    held = lax.dynamic_slice_in_dim(context, core * own_half, own_half, 0)[None]
    targets_swapped = None
    mask = 1
    while mask < seq_count:
        with jax.named_scope(f"gather_{mask}"):
            other = swap(held, mask)
        if targets_swapped is None:
            with jax.named_scope("swap_targets"):
                targets_swapped = swap(targets, core_mask)
            with jax.named_scope("swap_grads"):
                grad_swapped = swap(grad_out, core_mask)
        upper = bit_of(mask) == 1
        held = jnp.concatenate(
            [jnp.where(upper, other, held), jnp.where(upper, held, other)], axis=0
        )
        mask *= 2
    with jax.named_scope("gather_core"):
        other = swap(held, core_mask)
    held = jnp.stack(
        [jnp.where(core == 1, other, held), jnp.where(core == 1, held, other)], axis=1
    )
    context_all = held.reshape(context_rows, width)

    product = 2 * half_width * rows * width
    row_block = fixed((query_rows, width))
    with jax.named_scope("project_q"):
        queries = call(
            query_kernel,
            "project_q",
            high_count,
            [
                pl.BlockSpec((width, block), lambda i, core: (0, 2 * i + core[0])),
                row_block,
                row_block,
            ],
            pl.BlockSpec((block, rows), lambda i, core: (i, 0)),
            shaped(half_width, rows),
            product,
        )(core_index, w_query, targets, targets_swapped)
    with jax.named_scope("project_g"):
        grads = call(
            grad_kernel,
            "project_g",
            high_count,
            [
                pl.BlockSpec((block, width), lambda i, core: (2 * i + core[0], 0)),
                row_block,
                row_block,
            ],
            pl.BlockSpec((block, rows), lambda i, core: (i, 0)),
            shaped(half_width, rows),
            product,
        )(core_index, w_out, grad_out, grad_swapped)

    view_rows = query_rows * device_count // TVIEWS
    context_view = context_rows // CVIEWS
    firsts = jnp.stack([me, me ^ core_mask]) * query_rows // view_rows
    view_hot = firsts[:, None] == jnp.arange(TVIEWS)
    seen = jnp.sum(jnp.where(view_hot[:, :, None], visible[None], 0), axis=1)
    key_hot = jnp.arange(context_rows)[:, None] // context_view == jnp.arange(CVIEWS)
    seen = jnp.sum(jnp.where(key_hot[None], seen[:, None, :], 0), axis=2)
    bias = jnp.where(seen == 1, 0.0, -1e30).astype(F32)
    bias = jnp.broadcast_to(bias[:, :, None], (2, context_rows, 128))

    step_heads = 128 // head_size
    step_width = step_heads * head_size
    per_block = block // step_width
    steps = half_width // step_width

    def weight_spec(offset):
        def index(i, core):
            at = i + offset
            return (0, (2 * (at // per_block) + core[0]) * per_block + at % per_block)

        return pl.BlockSpec((width, step_width), index)

    def head_spec(offset):
        return pl.BlockSpec((step_width, rows), lambda i, core: (i + offset, 0))

    def kv_spec(offset):
        return pl.BlockSpec((2, step_width, context_rows), lambda i, core: (0, i + offset, 0))

    def probs_spec(offset):
        return pl.BlockSpec((step_heads, context_rows, rows), lambda i, core: (i + offset, 0, 0))

    attention = 8 * half_width * rows * context_rows
    with jax.named_scope("attend"):
        key_values, probs, attended, wo_term = call(
            partial(attend_kernel, step_heads, score_scale),
            "attend",
            steps,
            [
                fixed((context_rows, width)),
                weight_spec(0),
                weight_spec(0),
                head_spec(0),
                row_block,
                row_block,
                fixed((2, context_rows, 128)),
            ],
            [
                kv_spec(0),
                probs_spec(0),
                head_spec(0),
                pl.BlockSpec((step_width, width), lambda i, core: (i, 0)),
            ],
            [
                shaped(2, half_width, context_rows),
                shaped(half_width // head_size, context_rows, rows),
                shaped(half_width, rows),
                shaped(half_width, width),
            ],
            product + attention,
        )(core_index, context_all, w_key, w_value, queries, grad_out, grad_swapped, bias)

    def back(part, prior, earlier):
        offset = part * per_block
        qg_spec = pl.BlockSpec((step_width, query_rows), lambda i, core: (i + offset, 0))
        in_specs = [
            weight_spec(offset),
            weight_spec(offset),
            head_spec(offset),
            head_spec(offset),
            kv_spec(offset),
            probs_spec(offset),
            head_spec(offset),
            row_block,
            row_block,
            fixed((context_rows, width)),
        ]
        operands = [
            core_index,
            w_key,
            w_value,
            queries,
            grads,
            key_values,
            probs,
            attended,
            targets,
            targets_swapped,
            prior,
        ]
        kernel = partial(back_kernel, step_heads, score_scale)
        aliases = {}
        if earlier is not None:
            inner = kernel

            def kernel(*refs):
                return inner(*refs[:11], *refs[13:])

            in_specs = in_specs + [pl.BlockSpec(memory_space=pl.ANY)] * 2
            operands = operands + list(earlier)
            aliases = {11: 0, 12: 1}
        return call(
            kernel,
            "back",
            per_block,
            in_specs,
            [
                qg_spec,
                qg_spec,
                pl.BlockSpec((width, step_width), lambda i, core: (0, i)),
                pl.BlockSpec((context_rows, width), lambda i, core: (0, 0)),
            ],
            [
                shaped(half_width, query_rows),
                shaped(half_width, query_rows),
                shaped(width, block),
                shaped(context_rows, width, dtype=F32),
            ],
            (product + attention) // high_count,
            aliases=aliases,
        )(*operands)

    high_masks = []
    mask = core_mask * high_count
    while mask > core_mask:
        high_masks.append(mask)
        mask //= 2
    seq_masks = []
    mask = seq_count // 2
    while mask >= 1:
        seq_masks.append(mask)
        mask //= 2
    all_masks = high_masks + seq_masks
    orders = [(high_masks[-1], seq_masks[-1]), (seq_masks[-1], high_masks[-1])]
    rest = seq_masks[-2::-1] + high_masks[:-1]
    high_bits = [2] * len(high_masks)
    seq_bits = [2] * len(seq_masks)

    def halve(array, masks, mask, label, last=False):
        axis = masks.index(mask)
        bit = bit_of(mask)
        sent = lax.dynamic_index_in_dim(array, 1 - bit, axis, keepdims=False)
        kept = lax.dynamic_index_in_dim(array, bit, axis, keepdims=False)
        with jax.named_scope(label):
            moved = swap(sent, mask)
        total = kept.astype(F32) + moved.astype(F32)
        left = masks[:axis] + masks[axis + 1 :]
        return (total if last else total.astype(BF16)), left

    def halve_twice(array, masks, which, label):
        for step, mask in enumerate(orders[which]):
            array, masks = halve(array, masks, mask, f"{label}_{step}")
        return array, masks

    def halve_rest(array, masks, label):
        for step, mask in enumerate(rest):
            array, masks = halve(array, masks, mask, f"{label}_{step}", step == len(rest) - 1)
        return array

    out_rows = width // device_count
    ctx_out = context_rows // device_count

    wo_split = wo_term.reshape(*high_bits, *seq_bits, out_rows, width)
    wo_one, masks = halve_twice(wo_split[..., :half_width], all_masks, 0, "wo_a")
    wo_two, _ = halve_twice(wo_split[..., half_width:], all_masks, 1, "wo_b")
    grad_wo = halve_rest(jnp.concatenate([wo_one, wo_two], axis=-1), masks, "wo")

    ctx_term = jnp.zeros((context_rows, width), F32)
    query_parts = None
    wq_parts = []
    core_masks = high_masks + [0] + seq_masks
    for part in range(high_count):
        with jax.named_scope(f"back_{part}"):
            *query_parts, wq_term, ctx_term = back(part, ctx_term, query_parts)
        wq_split = wq_term.reshape(*high_bits, 2, *seq_bits, out_rows, block)
        wq_part, wq_masks = halve_twice(wq_split, core_masks, part % 2, f"wq_{part}")
        wq_parts.append(wq_part)

    ctx_split = ctx_term.reshape(high_count, 2, seq_count, ctx_out, width)
    ctx_kept = lax.dynamic_index_in_dim(ctx_split, core, 1, keepdims=False)
    ctx_sent = lax.dynamic_index_in_dim(ctx_split, 1 - core, 1, keepdims=False).astype(BF16)
    with jax.named_scope("ctx_core"):
        ctx_moved = swap(ctx_sent, core_mask)
    ctx_pair = (ctx_kept + ctx_moved.astype(F32)).astype(BF16)
    ctx_pair = ctx_pair.reshape(*high_bits, *seq_bits, ctx_out, width)
    ctx_pair, masks = halve_twice(ctx_pair, all_masks, 0, "ctx")
    ctx_pair = jnp.moveaxis(ctx_pair.reshape(*ctx_pair.shape[:-1], 2, half_width), -2, 0)
    ctx_pair = jnp.moveaxis(ctx_pair, 0, len(high_masks) - 1)
    tail = jnp.concatenate([jnp.concatenate(wq_parts, axis=-1), ctx_pair], axis=-2)
    tail = halve_rest(tail, wq_masks, "tail")

    mine = lax.dynamic_index_in_dim(tail[:, :out_rows], core, 0, keepdims=False)
    sent = lax.dynamic_index_in_dim(tail[:, :out_rows], 1 - core, 0, keepdims=False)
    with jax.named_scope("wq_core"):
        theirs = swap(sent, core_mask)
    pieces = []
    for part in range(high_count):
        cut = slice(part * block, (part + 1) * block)
        pieces.append(jnp.where(core == 0, mine[:, cut], theirs[:, cut]))
        pieces.append(jnp.where(core == 0, theirs[:, cut], mine[:, cut]))
    grad_wq = jnp.concatenate(pieces, axis=1)
    d_context = jnp.concatenate([tail[0, out_rows:], tail[1, out_rows:]], axis=1).astype(BF16)

    with jax.named_scope("query_core"):
        returned = swap(query_parts[1], core_mask)
    with jax.named_scope("targets_out"):
        d_targets = call(
            targets_kernel,
            "targets_out",
            high_count,
            [
                pl.BlockSpec((block, query_rows), lambda i, core: (i, 0)),
                pl.BlockSpec((block, query_rows), lambda i, core: (i, 0)),
                pl.BlockSpec((width, block), lambda i, core: (0, 2 * i + core[0])),
                pl.BlockSpec((width, block), lambda i, core: (0, 2 * i + 1 - core[0])),
            ],
            fixed((query_rows, width)),
            shaped(query_rows, width),
            product,
            scratch=[pltpu.VMEM((query_rows, width), F32)],
        )(core_index, query_parts[0], returned, w_query, w_query)
    return (d_targets, d_context, grad_wq, grad_wo)


def solution(mesh):
    in_specs = (
        P(AXES, None),
        P("seq", None),
        P(),
        P(),
        P(),
        P(),
        P(),
        P(AXES, None),
    )
    out_specs = (P(AXES, None), P(AXES, None), P(AXES, None), P(AXES, None))
    return jax.shard_map(
        on_device, mesh=mesh, in_specs=in_specs, out_specs=out_specs, check_vma=False
    )
```

```python
from functools import partial

import jax
import jax.numpy as jnp
from jax import lax
from jax.experimental import pallas as pl
from jax.experimental.pallas import tpu as pltpu
from jax.sharding import PartitionSpec as P


HEADS = 16
TVIEWS = 8
CVIEWS = 16
AXES = ("grp", "seq")

F32 = jnp.float32
BF16 = jnp.bfloat16


def dot(left, right, dims):
    return lax.dot_general(left, right, (dims, ((), ())), preferred_element_type=F32)


def query_kernel(core_ref, weight_ref, own_ref, partner_ref, out_ref):
    rows = own_ref.shape[0]
    weight = weight_ref[...]
    out_ref[:, :rows] = dot(own_ref[...], weight, ((1,), (0,))).astype(BF16).T
    out_ref[:, rows:] = dot(partner_ref[...], weight, ((1,), (0,))).astype(BF16).T


def grad_kernel(core_ref, weight_ref, own_ref, partner_ref, out_ref):
    rows = own_ref.shape[0]
    weight = weight_ref[...]
    out_ref[:, :rows] = dot(weight, own_ref[...], ((1,), (1,))).astype(BF16)
    out_ref[:, rows:] = dot(weight, partner_ref[...], ((1,), (1,))).astype(BF16)


def attend_kernel(
    heads,
    scale,
    core_ref,
    context_ref,
    wk_ref,
    wv_ref,
    q_ref,
    own_ref,
    partner_ref,
    bias_ref,
    kv_ref,
    probs_ref,
    att_ref,
    wo_ref,
):
    block_rows = own_ref.shape[0]
    keys = context_ref.shape[0]
    size = q_ref.shape[0] // heads
    context = context_ref[...]
    key_block = (dot(context, wk_ref[...], ((1,), (0,))).astype(BF16).astype(F32) * scale).astype(
        BF16
    )
    value_block = dot(context, wv_ref[...], ((1,), (0,))).astype(BF16)
    kv_ref[0] = key_block.T
    kv_ref[1] = value_block.T
    lane = lax.broadcasted_iota(jnp.int32, (keys, 2 * block_rows), 1)
    bias = jnp.where(lane < block_rows, bias_ref[0][:, :1], bias_ref[1][:, :1])
    for head in range(heads):
        part = pl.ds(head * size, size)
        scores = dot(kv_ref[0, part, :].T, q_ref[part, :], ((1,), (0,))) + bias
        row_max = jnp.max(scores, axis=0, keepdims=True)
        unnormed = jnp.exp(scores - row_max)
        row_sum = jnp.sum(unnormed, axis=0, keepdims=True)
        probs = (unnormed * (1.0 / row_sum)).astype(BF16)
        probs_ref[head] = probs
        att_ref[part, :] = dot(kv_ref[1, part, :], probs, ((1,), (0,))).astype(BF16)
    total = dot(att_ref[:, :block_rows], own_ref[...], ((1,), (0,)))
    total += dot(att_ref[:, block_rows:], partner_ref[...], ((1,), (0,)))
    wo_ref[...] = total.astype(BF16)


def back_kernel(
    heads,
    scale,
    core_ref,
    wk_ref,
    wv_ref,
    q_ref,
    g_ref,
    kv_ref,
    probs_ref,
    att_ref,
    own_ref,
    partner_ref,
    qg_own_ref,
    qg_partner_ref,
    wq_ref,
    ctx_ref,
    prior_ref=None,
):
    block_rows = own_ref.shape[0]
    size = q_ref.shape[0] // heads
    key_parts, value_parts = [], []
    for head in range(heads):
        part = pl.ds(head * size, size)
        grad = g_ref[part, :]
        probs = probs_ref[head]
        row_dot = jnp.sum(att_ref[part, :].astype(F32) * grad.astype(F32), axis=0, keepdims=True)
        grad_scores = dot(kv_ref[1, part, :].T, grad, ((1,), (0,)))
        value_parts.append(dot(grad, probs, ((1,), (1,))))
        logits = (probs.astype(F32) * (grad_scores - row_dot)).astype(BF16)
        query_grad = dot(kv_ref[0, part, :], logits, ((1,), (0,))).astype(BF16)
        qg_own_ref[part, :] = query_grad[:, :block_rows]
        qg_partner_ref[part, :] = query_grad[:, block_rows:]
        key_parts.append(dot(q_ref[part, :], logits, ((1,), (1,))) * scale)
    weight = dot(qg_own_ref[...], own_ref[...], ((1,), (0,)))
    weight += dot(qg_partner_ref[...], partner_ref[...], ((1,), (0,)))
    wq_ref[...] = weight.astype(BF16).T
    key_grad = jnp.concatenate(key_parts, axis=0).astype(BF16).T
    value_grad = jnp.concatenate(value_parts, axis=0).astype(BF16).T
    term = dot(key_grad, wk_ref[...], ((1,), (1,))) + dot(value_grad, wv_ref[...], ((1,), (1,)))

    @pl.when(pl.program_id(0) == 0)
    def _():
        ctx_ref[...] = term if prior_ref is None else prior_ref[...] + term

    @pl.when(pl.program_id(0) > 0)
    def _():
        ctx_ref[...] += term


def targets_kernel(core_ref, mine_ref, theirs_ref, wq_mine_ref, wq_theirs_ref, out_ref, acc_ref):
    term = dot(mine_ref[...], wq_mine_ref[...], ((0,), (1,)))
    term += dot(theirs_ref[...], wq_theirs_ref[...], ((0,), (1,)))
    step = pl.program_id(0)

    @pl.when(step == 0)
    def _():
        acc_ref[...] = term

    @pl.when(step > 0)
    def _():
        acc_ref[...] += term

    @pl.when(step == pl.num_programs(0) - 1)
    def _():
        out_ref[...] = acc_ref[...].astype(BF16)


def fixed(shape):
    return pl.BlockSpec(
        shape, lambda i, core: (0,) * len(shape), pipeline_mode=pl.Buffered(buffer_count=1)
    )


def call(kernel, steps, in_specs, out_specs, out_shape, flops, scratch=(), aliases=None):
    return pl.pallas_call(
        kernel,
        grid_spec=pltpu.PrefetchScalarGridSpec(
            num_scalar_prefetch=1,
            grid=(steps,),
            in_specs=in_specs,
            out_specs=out_specs,
            scratch_shapes=scratch,
        ),
        out_shape=out_shape,
        input_output_aliases=aliases or {},
        cost_estimate=pl.CostEstimate(flops=flops, bytes_accessed=4 << 20, transcendentals=0),
    )


def on_device(targets, context, w_query, w_key, w_value, w_out, visible, grad_out):
    query_rows, width = targets.shape
    head_size = width // HEADS
    score_scale = head_size ** (-0.5)
    grp_count = lax.axis_size("grp")
    seq_count = lax.axis_size("seq")
    device_count = grp_count * seq_count
    grp = lax.axis_index("grp")
    seq = lax.axis_index("seq")
    me = grp * seq_count + seq
    core = grp % 2
    core_mask = seq_count
    high_count = grp_count // 2
    half_width = width // 2
    block = width // grp_count
    context_rows = context.shape[0] * seq_count
    rows = 2 * query_rows
    core_index = core.reshape(1).astype(jnp.int32)

    def swap(array, mask):
        return lax.ppermute(array, AXES, [(i, i ^ mask) for i in range(device_count)])

    def bit_of(mask):
        return (me // mask) % 2

    def shaped(*shape, dtype=BF16):
        return jax.ShapeDtypeStruct(shape, dtype)

    own_half = context.shape[0] // 2
    held = lax.dynamic_slice_in_dim(context, core * own_half, own_half, 0)[None]
    targets_swapped = None
    mask = 1
    while mask < seq_count:
        other = swap(held, mask)
        if targets_swapped is None:
            targets_swapped = swap(targets, core_mask)
            grad_swapped = swap(grad_out, core_mask)
        upper = bit_of(mask) == 1
        held = jnp.concatenate(
            [jnp.where(upper, other, held), jnp.where(upper, held, other)], axis=0
        )
        mask *= 2
    other = swap(held, core_mask)
    held = jnp.stack(
        [jnp.where(core == 1, other, held), jnp.where(core == 1, held, other)], axis=1
    )
    context_all = held.reshape(context_rows, width)

    product = 2 * half_width * rows * width
    row_block = fixed((query_rows, width))
    queries = call(
        query_kernel,
        high_count,
        [pl.BlockSpec((width, block), lambda i, core: (0, 2 * i + core[0])), row_block, row_block],
        pl.BlockSpec((block, rows), lambda i, core: (i, 0)),
        shaped(half_width, rows),
        product,
    )(core_index, w_query, targets, targets_swapped)
    grads = call(
        grad_kernel,
        high_count,
        [pl.BlockSpec((block, width), lambda i, core: (2 * i + core[0], 0)), row_block, row_block],
        pl.BlockSpec((block, rows), lambda i, core: (i, 0)),
        shaped(half_width, rows),
        product,
    )(core_index, w_out, grad_out, grad_swapped)

    view_rows = query_rows * device_count // TVIEWS
    context_view = context_rows // CVIEWS
    firsts = jnp.stack([me, me ^ core_mask]) * query_rows // view_rows
    view_hot = firsts[:, None] == jnp.arange(TVIEWS)
    seen = jnp.sum(jnp.where(view_hot[:, :, None], visible[None], 0), axis=1)
    key_hot = jnp.arange(context_rows)[:, None] // context_view == jnp.arange(CVIEWS)
    seen = jnp.sum(jnp.where(key_hot[None], seen[:, None, :], 0), axis=2)
    bias = jnp.where(seen == 1, 0.0, -1e30).astype(F32)
    bias = jnp.broadcast_to(bias[:, :, None], (2, context_rows, 128))

    step_heads = 128 // head_size
    step_width = step_heads * head_size
    per_block = block // step_width
    steps = half_width // step_width

    def weight_spec(offset):
        def index(i, core):
            at = i + offset
            return (0, (2 * (at // per_block) + core[0]) * per_block + at % per_block)

        return pl.BlockSpec((width, step_width), index)

    def head_spec(offset):
        return pl.BlockSpec((step_width, rows), lambda i, core: (i + offset, 0))

    def kv_spec(offset):
        return pl.BlockSpec((2, step_width, context_rows), lambda i, core: (0, i + offset, 0))

    def probs_spec(offset):
        return pl.BlockSpec((step_heads, context_rows, rows), lambda i, core: (i + offset, 0, 0))

    attention = 8 * half_width * rows * context_rows
    key_values, probs, attended, wo_term = call(
        partial(attend_kernel, step_heads, score_scale),
        steps,
        [
            fixed((context_rows, width)),
            weight_spec(0),
            weight_spec(0),
            head_spec(0),
            row_block,
            row_block,
            fixed((2, context_rows, 128)),
        ],
        [
            kv_spec(0),
            probs_spec(0),
            head_spec(0),
            pl.BlockSpec((step_width, width), lambda i, core: (i, 0)),
        ],
        [
            shaped(2, half_width, context_rows),
            shaped(half_width // head_size, context_rows, rows),
            shaped(half_width, rows),
            shaped(half_width, width),
        ],
        product + attention,
    )(core_index, context_all, w_key, w_value, queries, grad_out, grad_swapped, bias)

    def back(part, prior, earlier):
        offset = part * per_block
        qg_spec = pl.BlockSpec((step_width, query_rows), lambda i, core: (i + offset, 0))
        in_specs = [
            weight_spec(offset),
            weight_spec(offset),
            head_spec(offset),
            head_spec(offset),
            kv_spec(offset),
            probs_spec(offset),
            head_spec(offset),
            row_block,
            row_block,
        ]
        operands = [
            core_index,
            w_key,
            w_value,
            queries,
            grads,
            key_values,
            probs,
            attended,
            targets,
            targets_swapped,
        ]
        kernel = partial(back_kernel, step_heads, score_scale)
        aliases = {}
        if earlier is not None:
            inner = kernel

            def kernel(*refs):
                return inner(*refs[:10], *refs[13:], prior_ref=refs[12])

            in_specs = in_specs + [pl.BlockSpec(memory_space=pl.ANY)] * 2
            in_specs.append(fixed((context_rows, width)))
            operands = operands + list(earlier) + [prior]
            aliases = {10: 0, 11: 1}
        return call(
            kernel,
            per_block,
            in_specs,
            [
                qg_spec,
                qg_spec,
                pl.BlockSpec((width, step_width), lambda i, core: (0, i)),
                pl.BlockSpec((context_rows, width), lambda i, core: (0, 0)),
            ],
            [
                shaped(half_width, query_rows),
                shaped(half_width, query_rows),
                shaped(width, block),
                shaped(context_rows, width, dtype=F32),
            ],
            (product + attention) // high_count,
            aliases=aliases,
        )(*operands)

    high_masks = []
    mask = core_mask * high_count
    while mask > core_mask:
        high_masks.append(mask)
        mask //= 2
    seq_masks = []
    mask = seq_count // 2
    while mask >= 1:
        seq_masks.append(mask)
        mask //= 2
    all_masks = high_masks + seq_masks
    core_masks = high_masks + [0] + seq_masks
    high_bits = [2] * len(high_masks)
    seq_bits = [2] * len(seq_masks)
    order = [high_masks[-1], seq_masks[-1]] + seq_masks[-2::-1] + high_masks[:-1]
    stages = [tuple(order[at : at + 2]) for at in range(0, len(order), 2)]

    def exchange(array, masks, stage, last=False):
        def piece(flips):
            part = array
            for mask, flip in sorted(zip(stage, flips), key=lambda one: -masks.index(one[0])):
                at = (bit_of(mask) + flip) % 2
                part = lax.dynamic_index_in_dim(part, at, masks.index(mask), keepdims=False)
            return part

        moved = []
        for way in range(1, 2 ** len(stage)):
            flips = [way >> at & 1 for at in range(len(stage))]
            target = sum(mask for mask, flip in zip(stage, flips) if flip)
            moved.append(swap(piece(flips), target))
        total = piece([0] * len(stage)).astype(F32)
        for one in moved:
            total = total + one.astype(F32)
        left = [mask for mask in masks if mask not in stage]
        return (total if last else total.astype(BF16)), left

    def exchange_rest(array, masks):
        for at, stage in enumerate(stages[1:]):
            array, masks = exchange(array, masks, stage, at == len(stages) - 2)
        return array

    out_rows = width // device_count
    ctx_out = context_rows // device_count

    wo_split = wo_term.reshape(*high_bits, *seq_bits, out_rows, width)
    wo_part, left_masks = exchange(wo_split, all_masks, stages[0])

    ctx_term = None
    query_parts = None
    wq_parts = []
    for part in range(high_count):
        *query_parts, wq_term, ctx_term = back(part, ctx_term, query_parts)
        wq_split = wq_term.reshape(*high_bits, 2, *seq_bits, out_rows, block)
        wq_part, _ = exchange(wq_split, core_masks, stages[0])
        wq_parts.append(wq_part)

    ctx_split = ctx_term.reshape(high_count, 2, seq_count, ctx_out, width)
    ctx_kept = lax.dynamic_index_in_dim(ctx_split, core, 1, keepdims=False)
    ctx_sent = lax.dynamic_index_in_dim(ctx_split, 1 - core, 1, keepdims=False).astype(BF16)
    ctx_moved = swap(ctx_sent, core_mask)
    ctx_pair = (ctx_kept + ctx_moved.astype(F32)).astype(BF16)
    ctx_pair = ctx_pair.reshape(*high_bits, *seq_bits, ctx_out, width)
    ctx_pair, _ = exchange(ctx_pair, all_masks, stages[0])

    at_core = len(high_masks) - 1
    early = [wo_part[..., cut * block : (cut + 1) * block] for cut in range(width // block)]
    for wq_part in wq_parts[:-1]:
        early += [lax.index_in_dim(wq_part, which, at_core, keepdims=False) for which in (0, 1)]
    early = exchange_rest(jnp.concatenate(early, axis=-2), left_masks)
    late = [lax.index_in_dim(wq_parts[-1], which, at_core, keepdims=False) for which in (0, 1)]
    late += [ctx_pair[..., cut * block : (cut + 1) * block] for cut in range(width // block)]
    late = exchange_rest(jnp.concatenate(late, axis=-2), left_masks)

    cuts = width // block
    grad_wo = jnp.concatenate(
        [early[cut * out_rows : (cut + 1) * out_rows] for cut in range(cuts)], axis=1
    )
    wq_sums = early[cuts * out_rows :].reshape(high_count - 1, 2, out_rows, block)
    wq_sums = jnp.concatenate([wq_sums, late[: 2 * out_rows].reshape(1, 2, out_rows, block)])
    sent = lax.dynamic_index_in_dim(wq_sums, 1 - core, 1, keepdims=False)
    mine = lax.dynamic_index_in_dim(wq_sums, core, 1, keepdims=False)
    theirs = swap(sent, core_mask)
    pieces = []
    for part in range(high_count):
        pieces.append(jnp.where(core == 0, mine[part], theirs[part]))
        pieces.append(jnp.where(core == 0, theirs[part], mine[part]))
    grad_wq = jnp.concatenate(pieces, axis=1)
    ctx_sums = late[2 * out_rows :]
    d_context = jnp.concatenate(
        [ctx_sums[cut * ctx_out : (cut + 1) * ctx_out] for cut in range(cuts)], axis=1
    ).astype(BF16)

    returned = swap(query_parts[1], core_mask)
    d_targets = call(
        targets_kernel,
        high_count,
        [
            pl.BlockSpec((block, query_rows), lambda i, core: (i, 0)),
            pl.BlockSpec((block, query_rows), lambda i, core: (i, 0)),
            pl.BlockSpec((width, block), lambda i, core: (0, 2 * i + core[0])),
            pl.BlockSpec((width, block), lambda i, core: (0, 2 * i + 1 - core[0])),
        ],
        fixed((query_rows, width)),
        shaped(query_rows, width),
        product,
        scratch=[pltpu.VMEM((query_rows, width), F32)],
    )(core_index, query_parts[0], returned, w_query, w_query)
    return (d_targets, d_context, grad_wq, grad_wo)


def solution(mesh):
    in_specs = (
        P(AXES, None),
        P("seq", None),
        P(),
        P(),
        P(),
        P(),
        P(),
        P(AXES, None),
    )
    out_specs = (P(AXES, None), P(AXES, None), P(AXES, None), P(AXES, None))

    return jax.shard_map(
        on_device, mesh=mesh, in_specs=in_specs, out_specs=out_specs, check_vma=False
    )
```

```python
from functools import partial

import jax
import jax.numpy as jnp
from jax import lax
from jax.experimental import pallas as pl
from jax.experimental.pallas import tpu as pltpu
from jax.sharding import PartitionSpec as P


HEADS = 16
TVIEWS = 8
CVIEWS = 16
AXES = ("grp", "seq")
GROUP = 2

F32 = jnp.float32
BF16 = jnp.bfloat16


def dot(left, right, dims):
    return lax.dot_general(left, right, (dims, ((), ())), preferred_element_type=F32)


def owned(core_ref, at, size, block):
    return pl.ds(pl.multiple_of((2 * (at // block) + core_ref[0]) * block + at % block, size), size)


def query_kernel(block, core_ref, weight_ref, own_ref, partner_ref, out_ref):
    rows = own_ref.shape[0]
    for at in range(0, out_ref.shape[0], block):
        weight = weight_ref[:, owned(core_ref, at, block, block)]
        part = pl.ds(at, block)
        out_ref[part, :rows] = dot(own_ref[...], weight, ((1,), (0,))).astype(BF16).T
        out_ref[part, rows:] = dot(partner_ref[...], weight, ((1,), (0,))).astype(BF16).T


def grad_kernel(block, core_ref, weight_ref, own_ref, partner_ref, out_ref):
    rows = own_ref.shape[0]
    for at in range(0, out_ref.shape[0], block):
        weight = weight_ref[owned(core_ref, at, block, block), :]
        part = pl.ds(at, block)
        out_ref[part, :rows] = dot(weight, own_ref[...], ((1,), (1,))).astype(BF16)
        out_ref[part, rows:] = dot(weight, partner_ref[...], ((1,), (1,))).astype(BF16)


def attend_kernel(
    block,
    size,
    scale,
    core_ref,
    context_ref,
    wk_ref,
    wv_ref,
    q_ref,
    own_ref,
    partner_ref,
    bias_ref,
    kv_ref,
    probs_ref,
    att_ref,
    wo_ref,
):
    block_rows = own_ref.shape[0]
    rows = 2 * block_rows
    width = GROUP * size
    context = context_ref[...]
    bias = bias_ref[...]
    lane = lax.broadcasted_iota(jnp.int32, (16, rows), 1)
    line = lax.broadcasted_iota(jnp.int32, (16, rows), 0)
    marks = jnp.where(lane // block_rows == line, 1.0, 0.0).astype(BF16)

    def keys_values(at):
        cols = owned(core_ref, at, width, block)
        weight = jnp.concatenate([wk_ref[:, cols], wv_ref[:, cols]], axis=1)
        both = dot(context, weight, ((1,), (0,))).astype(BF16)
        key_part = (both[:, :width].astype(F32) * scale).astype(BF16)
        kv_ref[0, pl.ds(at, width), :] = key_part.T
        kv_ref[1, pl.ds(at, width), :] = both[:, width:].T

    def out_product(at, depth):
        part = pl.ds(at, depth)
        total = dot(att_ref[part, :block_rows], own_ref[...], ((1,), (0,)))
        total += dot(att_ref[part, block_rows:], partner_ref[...], ((1,), (0,)))
        wo_ref[part, :] = total.astype(BF16)

    half_width = q_ref.shape[0]
    keys_values(0)
    for at in range(0, half_width, width):
        if at + width < half_width:
            keys_values(at + width)
        for first in range(at, at + width, size):
            part = pl.ds(first, size)
            key_rows = jnp.concatenate([kv_ref[0, part, :], bias], axis=0)
            query_rows = jnp.concatenate([q_ref[part, :], marks], axis=0)
            scores = dot(key_rows.T, query_rows, ((1,), (0,)))
            row_max = jnp.max(scores, axis=0, keepdims=True)
            unnormed = jnp.exp(scores - row_max)
            row_sum = jnp.sum(unnormed, axis=0, keepdims=True)
            probs = (unnormed * (1.0 / row_sum)).astype(BF16)
            probs_ref[first // size] = probs
            att_ref[part, :] = dot(kv_ref[1, part, :], probs, ((1,), (0,))).astype(BF16)
        if (at // width) % 2 == 1:
            out_product(at - width, 2 * width)


def back_kernel(
    block,
    size,
    scale,
    core_ref,
    wk_ref,
    wv_ref,
    q_ref,
    g_ref,
    kv_ref,
    probs_ref,
    att_ref,
    qg_own_ref,
    qg_partner_ref,
    kept_ref,
    sent_ref,
    sum_ref,
):
    half_width = q_ref.shape[0]
    block_rows = qg_own_ref.shape[1]
    width = GROUP * size
    for at in range(0, half_width, width):
        key_parts, value_parts = [], []
        for first in range(at, at + width, size):
            part = pl.ds(first, size)
            grad = g_ref[part, :]
            probs = probs_ref[first // size]
            attended = att_ref[part, :].astype(F32)
            row_dot = jnp.sum(attended * grad.astype(F32), axis=0, keepdims=True)
            grad_scores = dot(kv_ref[1, part, :].T, grad, ((1,), (0,)))
            value_parts.append(dot(grad, probs, ((1,), (1,))))
            logits = (probs.astype(F32) * (grad_scores - row_dot)).astype(BF16)
            query_grad = dot(kv_ref[0, part, :], logits, ((1,), (0,))).astype(BF16)
            qg_own_ref[part, :] = query_grad[:, :block_rows]
            qg_partner_ref[part, :] = query_grad[:, block_rows:]
            key_parts.append(dot(q_ref[part, :], logits, ((1,), (1,))) * scale)
        cols = owned(core_ref, at, width, block)
        grads = jnp.concatenate(key_parts + value_parts, axis=0).astype(BF16).T
        weight = jnp.concatenate([wk_ref[:, cols], wv_ref[:, cols]], axis=1)
        term = dot(grads, weight, ((1,), (1,)))
        if at == 0:
            sum_ref[...] = term
        else:
            sum_ref[...] += term
    out_block = kept_ref.shape[1]
    for high in range(kept_ref.shape[0]):
        kept = pl.multiple_of((2 * high + core_ref[0]) * out_block, out_block)
        sent = pl.multiple_of((2 * high + 1 - core_ref[0]) * out_block, out_block)
        kept_ref[high] = sum_ref[pl.ds(kept, out_block), :]
        sent_ref[high] = sum_ref[pl.ds(sent, out_block), :].astype(BF16)


def weight_kernel(qg_own_ref, qg_partner_ref, own_ref, partner_ref, out_ref):
    step = min(256, qg_own_ref.shape[0])
    for at in range(0, qg_own_ref.shape[0], step):
        part = pl.ds(at, step)
        total = dot(qg_own_ref[part, :], own_ref[...], ((1,), (0,)))
        total += dot(qg_partner_ref[part, :], partner_ref[...], ((1,), (0,)))
        out_ref[:, part] = total.astype(BF16).T


def targets_kernel(block, core_ref, mine_ref, theirs_ref, weight_ref, out_ref):
    other_ref = [1 - core_ref[0]]
    total = None
    for at in range(0, mine_ref.shape[0], block):
        part = pl.ds(at, block)
        for source, core in ((mine_ref, core_ref), (theirs_ref, other_ref)):
            weight = weight_ref[:, owned(core, at, block, block)]
            term = dot(source[part, :].T, weight, ((1,), (1,)))
            total = term if total is None else total + term
    out_ref[...] = total.astype(BF16)


def on_device(targets, context, w_query, w_key, w_value, w_out, visible, grad_out):
    query_rows, width = targets.shape
    head_size = width // HEADS
    score_scale = head_size ** (-0.5)
    grp_count = lax.axis_size("grp")
    seq_count = lax.axis_size("seq")
    device_count = grp_count * seq_count
    grp = lax.axis_index("grp")
    seq = lax.axis_index("seq")
    me = grp * seq_count + seq
    core = grp % 2
    core_mask = seq_count
    high_count = grp_count // 2
    half_width = width // 2
    half_heads = HEADS // 2
    block = width // grp_count
    context_rows = context.shape[0] * seq_count
    rows = 2 * query_rows
    core_index = core.reshape(1).astype(jnp.int32)
    limit = (10 << 20) + 6 * 4 * context_rows * rows

    def swap(array, mask):
        return lax.ppermute(array, AXES, [(i, i ^ mask) for i in range(device_count)])

    def bit_of(mask):
        return (me // mask) % 2

    def call(kernel, operands, outs, flops, scratch=()):
        in_vmem = pl.BlockSpec(memory_space=pltpu.VMEM)
        scalar = pl.BlockSpec(memory_space=pltpu.SMEM)
        specs = [scalar if one is core_index else in_vmem for one in operands]
        return pl.pallas_call(
            kernel,
            in_specs=specs,
            out_specs=[in_vmem] * len(outs),
            out_shape=[jax.ShapeDtypeStruct(shape, kind) for shape, kind in outs],
            scratch_shapes=scratch,
            compiler_params=pltpu.CompilerParams(vmem_limit_bytes=limit),
            cost_estimate=pl.CostEstimate(flops=flops, bytes_accessed=1 << 20, transcendentals=0),
        )(*operands)

    own_half = context.shape[0] // 2
    held = lax.dynamic_slice_in_dim(context, core * own_half, own_half, 0)[None]
    targets_swapped = None
    mask = 1
    while mask < seq_count:
        other = swap(held, mask)
        if targets_swapped is None:
            targets_swapped = swap(targets, core_mask)
            grad_swapped = swap(grad_out, core_mask)
        upper = bit_of(mask) == 1
        held = jnp.concatenate(
            [jnp.where(upper, other, held), jnp.where(upper, held, other)], axis=0
        )
        mask *= 2
    other = swap(held, core_mask)
    held = jnp.stack(
        [jnp.where(core == 1, other, held), jnp.where(core == 1, held, other)], axis=1
    )
    context_all = held.reshape(context_rows, width)

    product = 2 * half_width * rows * width
    attention = 8 * half_width * rows * context_rows
    (queries,) = call(
        partial(query_kernel, block),
        [core_index, w_query, targets, targets_swapped],
        [((half_width, rows), BF16)],
        product,
    )
    (grads,) = call(
        partial(grad_kernel, block),
        [core_index, w_out, grad_out, grad_swapped],
        [((half_width, rows), BF16)],
        product,
    )

    view_rows = query_rows * device_count // TVIEWS
    context_view = context_rows // CVIEWS
    firsts = jnp.stack([me, me ^ core_mask]) * query_rows // view_rows
    view_hot = firsts[:, None] == jnp.arange(TVIEWS)
    seen = jnp.sum(jnp.where(view_hot[:, :, None], visible[None], 0), axis=1)
    key_hot = jnp.arange(context_rows)[:, None] // context_view == jnp.arange(CVIEWS)
    seen = jnp.sum(jnp.where(key_hot[None], seen[:, None, :], 0), axis=2)
    bias = jnp.where(seen == 1, 0.0, -1e30).astype(BF16)
    bias = jnp.concatenate([bias, jnp.zeros((14, context_rows), BF16)], axis=0)

    key_values, probs, attended, wo_term = call(
        partial(attend_kernel, block, head_size, score_scale),
        [core_index, context_all, w_key, w_value, queries, grad_out, grad_swapped, bias],
        [
            ((2, half_width, context_rows), BF16),
            ((half_heads, context_rows, rows), BF16),
            ((half_width, rows), BF16),
            ((half_width, width), BF16),
        ],
        product + attention,
    )

    high_masks = []
    mask = core_mask * high_count
    while mask > core_mask:
        high_masks.append(mask)
        mask //= 2
    seq_masks = []
    mask = seq_count // 2
    while mask >= 1:
        seq_masks.append(mask)
        mask //= 2
    all_masks = high_masks + seq_masks
    high_bits = [2] * len(high_masks)
    seq_bits = [2] * len(seq_masks)
    order = [high_masks[-1], seq_masks[-1]] + seq_masks[-2::-1] + high_masks[:-1]
    stages = [tuple(order[at : at + 2]) for at in range(0, len(order), 2)]

    def exchange(array, masks, stage, last=False):
        def piece(flips):
            part = array
            for mask, flip in sorted(zip(stage, flips), key=lambda one: -masks.index(one[0])):
                at = (bit_of(mask) + flip) % 2
                part = lax.dynamic_index_in_dim(part, at, masks.index(mask), keepdims=False)
            return part

        moved = []
        for way in range(1, 2 ** len(stage)):
            flips = [way >> at & 1 for at in range(len(stage))]
            target = sum(mask for mask, flip in zip(stage, flips) if flip)
            moved.append(swap(piece(flips), target))
        total = piece([0] * len(stage)).astype(F32)
        for one in moved:
            total = total + one.astype(F32)
        left = [mask for mask in masks if mask not in stage]
        return (total if last else total.astype(BF16)), left

    def exchange_rest(array, masks):
        for at, stage in enumerate(stages[1:]):
            array, masks = exchange(array, masks, stage, at == len(stages) - 2)
        return array

    out_rows = width // device_count
    ctx_out = context_rows // device_count

    wo_split = wo_term.reshape(*high_bits, *seq_bits, out_rows, width)
    wo_part, left_masks = exchange(wo_split, all_masks, stages[0])
    grad_wo = exchange_rest(wo_part, left_masks)

    query_own, query_partner, ctx_kept, ctx_sent = call(
        partial(back_kernel, block, head_size, score_scale),
        [core_index, w_key, w_value, queries, grads, key_values, probs, attended],
        [
            ((half_width, query_rows), BF16),
            ((half_width, query_rows), BF16),
            ((high_count, seq_count * ctx_out, width), F32),
            ((high_count, seq_count * ctx_out, width), BF16),
        ],
        product // 2 + attention,
        scratch=[pltpu.VMEM((context_rows, width), F32)],
    )
    ctx_moved = swap(ctx_sent, core_mask)
    (wq_term,) = call(
        weight_kernel,
        [query_own, query_partner, targets, targets_swapped],
        [((width, half_width), BF16)],
        product,
    )
    ctx_pair = (ctx_kept + ctx_moved.astype(F32)).astype(BF16)
    ctx_pair = ctx_pair.reshape(*high_bits, *seq_bits, ctx_out, width)
    wq_split = wq_term.reshape(high_count, 2, seq_count, out_rows, half_width)
    tail = [wq_split[:, which].reshape(*high_bits, *seq_bits, out_rows, half_width) for which in (0, 1)]
    tail += [ctx_pair[..., :half_width], ctx_pair[..., half_width:]]
    tail, _ = exchange(jnp.concatenate(tail, axis=-2), all_masks, stages[0])
    tail = exchange_rest(tail, left_masks)

    wq_sums = tail[: 2 * out_rows].reshape(2, out_rows, half_width)
    sent = lax.dynamic_index_in_dim(wq_sums, 1 - core, 0, keepdims=False)
    mine = lax.dynamic_index_in_dim(wq_sums, core, 0, keepdims=False)
    theirs = swap(sent, core_mask)
    pieces = []
    for at in range(0, half_width, block):
        pieces.append(jnp.where(core == 0, mine[:, at : at + block], theirs[:, at : at + block]))
        pieces.append(jnp.where(core == 0, theirs[:, at : at + block], mine[:, at : at + block]))
    grad_wq = jnp.concatenate(pieces, axis=1)
    ctx_sums = tail[2 * out_rows :]
    d_context = jnp.concatenate([ctx_sums[:ctx_out], ctx_sums[ctx_out:]], axis=1).astype(BF16)

    returned = swap(query_partner, core_mask)
    (d_targets,) = call(
        partial(targets_kernel, block),
        [core_index, query_own, returned, w_query],
        [((query_rows, width), BF16)],
        product,
    )
    return (d_targets, d_context, grad_wq, grad_wo)


def solution(mesh):
    in_specs = (
        P(AXES, None),
        P("seq", None),
        P(),
        P(),
        P(),
        P(),
        P(),
        P(AXES, None),
    )
    out_specs = (P(AXES, None), P(AXES, None), P(AXES, None), P(AXES, None))

    return jax.shard_map(
        on_device, mesh=mesh, in_specs=in_specs, out_specs=out_specs, check_vma=False
    )
```

```python
from functools import partial

import jax
import jax.numpy as jnp
from jax import lax
from jax.experimental import pallas as pl
from jax.experimental.pallas import tpu as pltpu
from jax.sharding import PartitionSpec as P


HEADS = 16
TVIEWS = 8
CVIEWS = 16
AXES = ("grp", "seq")
GROUP = 2

F32 = jnp.float32
BF16 = jnp.bfloat16


def dot(left, right, dims):
    return lax.dot_general(left, right, (dims, ((), ())), preferred_element_type=F32)


def owned(place_ref, at, size, block):
    return pl.ds(pl.multiple_of((2 * (at // block) + place_ref[0]) * block + at % block, size), size)


def query_kernel(block, place_ref, weight_ref, own_ref, partner_ref, out_ref, tokens, weights, sems):
    rows = partner_ref.shape[0]
    count = weights.shape[0]
    copies = []
    for at in range(count):
        part = owned(place_ref, at * block, block, block)
        copies.append(pltpu.make_async_copy(weight_ref.at[:, part], weights.at[at], sems.at[at]))
    copies.append(pltpu.make_async_copy(own_ref, tokens, sems.at[count]))
    for one in copies:
        one.start()
    for side, source in enumerate((partner_ref, tokens)):
        if side == 1:
            copies[count].wait()
        for at in range(count):
            if side == 0:
                copies[at].wait()
            term = dot(source[...], weights[at], ((1,), (0,))).astype(BF16).T
            out_ref[pl.ds(at * block, block), pl.ds((1 - side) * rows, rows)] = term


def grad_kernel(block, place_ref, weight_ref, own_ref, partner_ref, out_ref, tokens, weights, sems):
    rows = partner_ref.shape[0]
    count = weights.shape[0]
    copies = []
    for at in range(count):
        part = owned(place_ref, at * block, block, block)
        copies.append(pltpu.make_async_copy(weight_ref.at[part, :], weights.at[at], sems.at[at]))
    copies.append(pltpu.make_async_copy(own_ref, tokens, sems.at[count]))
    for one in copies:
        one.start()
    for side, source in enumerate((partner_ref, tokens)):
        if side == 1:
            copies[count].wait()
        for at in range(count):
            if side == 0:
                copies[at].wait()
            term = dot(weights[at], source[...], ((1,), (1,))).astype(BF16)
            out_ref[pl.ds(at * block, block), pl.ds((1 - side) * rows, rows)] = term


def fetch_kernel(block, group, place_ref, wk_ref, wv_ref, wkv_ref, sems):
    copies = []
    for at in range(wkv_ref.shape[0]):
        part = owned(place_ref, at * group, group, block)
        for which, source in enumerate((wk_ref, wv_ref)):
            target = wkv_ref.at[at, :, pl.ds(which * group, group)]
            copies.append(
                pltpu.make_async_copy(source.at[:, part], target, sems.at[2 * at + which])
            )
            copies[-1].start()
    for one in copies:
        one.wait()


def attend_kernel(
    size,
    scale,
    place_ref,
    mine_ref,
    other_ref,
    wkv_ref,
    q_ref,
    g_ref,
    bias_ref,
    own_ref,
    partner_ref,
    kv_ref,
    probs_ref,
    row_dot_ref,
    wo_ref,
    context_ref,
    att_ref,
    tokens,
    sems,
):
    half_width, rows = q_ref.shape
    block_rows = rows // 2
    width = GROUP * size
    moves = []
    for side, source in enumerate((own_ref, partner_ref)):
        moves.append(pltpu.make_async_copy(source, tokens.at[side], sems.at[side]))
        moves[-1].start()
    shards, half_rows = mine_ref.shape[:2]
    for at in range(shards):
        first = lax.bitwise_xor(place_ref[1], at) * 2 * half_rows
        mine = pl.multiple_of(first + place_ref[0] * half_rows, half_rows)
        other = pl.multiple_of(first + (1 - place_ref[0]) * half_rows, half_rows)
        context_ref[pl.ds(mine, half_rows), :] = mine_ref[at]
        context_ref[pl.ds(other, half_rows), :] = other_ref[at]
    context = context_ref[...]
    bias = bias_ref[...]
    lane = lax.broadcasted_iota(jnp.int32, (16, rows), 1)
    line = lax.broadcasted_iota(jnp.int32, (16, rows), 0)
    marks = jnp.where(lane // block_rows == line, 1.0, 0.0).astype(BF16)

    def keys_values(at):
        step = at // width
        both = dot(context, wkv_ref[step], ((1,), (0,))).astype(BF16)
        key_part = (both[:, :width].astype(F32) * scale).astype(BF16)
        kv_ref[0, pl.ds(at, width), :] = key_part.T
        kv_ref[1, pl.ds(at, width), :] = both[:, width:].T

    keys_values(0)
    for at in range(0, half_width, width):
        if at + width < half_width:
            keys_values(at + width)
        for first in range(at, at + width, size):
            part = pl.ds(first, size)
            key_rows = jnp.concatenate([kv_ref[0, part, :], bias], axis=0)
            query_rows = jnp.concatenate([q_ref[part, :], marks], axis=0)
            scores = dot(key_rows.T, query_rows, ((1,), (0,)))
            row_max = jnp.max(scores, axis=0, keepdims=True)
            unnormed = jnp.exp(scores - row_max)
            row_sum = jnp.sum(unnormed, axis=0, keepdims=True)
            probs = (unnormed * (1.0 / row_sum)).astype(BF16)
            probs_ref[first // size] = probs
            attended = dot(kv_ref[1, part, :], probs, ((1,), (0,))).astype(BF16)
            att_ref[part, :] = attended
            row_dot = attended.astype(F32) * g_ref[part, :].astype(F32)
            row_dot_ref[pl.ds(first // size, 1), :] = jnp.sum(row_dot, axis=0, keepdims=True)
        if (at // width) % 2 == 1:
            if at == width:
                for move in moves:
                    move.wait()
            part = pl.ds(at - width, 2 * width)
            total = dot(att_ref[part, :block_rows], tokens[0], ((1,), (0,)))
            total += dot(att_ref[part, block_rows:], tokens[1], ((1,), (0,)))
            wo_ref[part, :] = total.astype(BF16)


def back_kernel(
    size,
    scale,
    place_ref,
    wkv_ref,
    q_ref,
    g_ref,
    kv_ref,
    probs_ref,
    row_dot_ref,
    qg_own_ref,
    qg_partner_ref,
    kept_ref,
    sent_ref,
    sum_ref,
):
    half_width = q_ref.shape[0]
    block_rows = qg_own_ref.shape[1]
    width = GROUP * size
    for at in range(0, half_width, width):
        key_parts, value_parts = [], []
        for first in range(at, at + width, size):
            part = pl.ds(first, size)
            grad = g_ref[part, :]
            probs = probs_ref[first // size]
            row_dot = row_dot_ref[pl.ds(first // size, 1), :]
            grad_scores = dot(kv_ref[1, part, :].T, grad, ((1,), (0,)))
            value_parts.append(dot(grad, probs, ((1,), (1,))))
            logits = (probs.astype(F32) * (grad_scores - row_dot)).astype(BF16)
            query_grad = dot(kv_ref[0, part, :], logits, ((1,), (0,))).astype(BF16)
            qg_own_ref[part, :] = query_grad[:, :block_rows]
            qg_partner_ref[part, :] = query_grad[:, block_rows:]
            key_parts.append(dot(q_ref[part, :], logits, ((1,), (1,))) * scale)
        grads = jnp.concatenate(key_parts + value_parts, axis=0).astype(BF16).T
        term = dot(grads, wkv_ref[at // width], ((1,), (1,)))
        if at == 0:
            sum_ref[...] = term
        else:
            sum_ref[...] += term
    out_block = kept_ref.shape[1]
    for high in range(kept_ref.shape[0]):
        kept = pl.multiple_of((2 * high + place_ref[0]) * out_block, out_block)
        sent = pl.multiple_of((2 * high + 1 - place_ref[0]) * out_block, out_block)
        kept_ref[high] = sum_ref[pl.ds(kept, out_block), :]
        sent_ref[high] = sum_ref[pl.ds(sent, out_block), :].astype(BF16)


def weight_kernel(qg_own_ref, qg_partner_ref, own_ref, partner_ref, out_ref):
    step = min(256, qg_own_ref.shape[0])
    for at in range(0, qg_own_ref.shape[0], step):
        part = pl.ds(at, step)
        total = dot(qg_own_ref[part, :], own_ref[...], ((1,), (0,)))
        total += dot(qg_partner_ref[part, :], partner_ref[...], ((1,), (0,)))
        out_ref[:, part] = total.astype(BF16).T


def targets_kernel(block, place_ref, mine_ref, theirs_ref, weight_ref, out_ref):
    other_ref = [1 - place_ref[0]]
    total = None
    for at in range(0, mine_ref.shape[0], block):
        part = pl.ds(at, block)
        for source, core in ((mine_ref, place_ref), (theirs_ref, other_ref)):
            weight = weight_ref[:, owned(core, at, block, block)]
            term = dot(source[part, :].T, weight, ((1,), (1,)))
            total = term if total is None else total + term
    out_ref[...] = total.astype(BF16)


def on_device(targets, context, w_query, w_key, w_value, w_out, visible, grad_out):
    query_rows, width = targets.shape
    head_size = width // HEADS
    score_scale = head_size ** (-0.5)
    grp_count = lax.axis_size("grp")
    seq_count = lax.axis_size("seq")
    device_count = grp_count * seq_count
    grp = lax.axis_index("grp")
    seq = lax.axis_index("seq")
    me = grp * seq_count + seq
    core = grp % 2
    core_mask = seq_count
    high_count = grp_count // 2
    half_width = width // 2
    half_heads = HEADS // 2
    block = width // grp_count
    context_rows = context.shape[0] * seq_count
    rows = 2 * query_rows
    place = jnp.stack([core, seq]).astype(jnp.int32)
    limit = (14 << 20) + 6 * 4 * context_rows * rows

    def swap(array, mask):
        return lax.ppermute(array, AXES, [(i, i ^ mask) for i in range(device_count)])

    def bit_of(mask):
        return (me // mask) % 2

    def call(kernel, operands, outs, flops, scratch=(), fetched=()):
        in_vmem = pl.BlockSpec(memory_space=pltpu.VMEM)
        scalar = pl.BlockSpec(memory_space=pltpu.SMEM)
        anywhere = pl.BlockSpec(memory_space=pltpu.HBM)
        specs = [scalar if one is place else in_vmem for one in operands]
        operands = list(operands)
        for at in fetched:
            specs[at] = anywhere
            operands[at] = pltpu.with_memory_space_constraint(operands[at], pltpu.HBM)
        return pl.pallas_call(
            kernel,
            in_specs=specs,
            out_specs=[in_vmem] * len(outs),
            out_shape=[jax.ShapeDtypeStruct(shape, kind) for shape, kind in outs],
            scratch_shapes=scratch,
            compiler_params=pltpu.CompilerParams(vmem_limit_bytes=limit),
            cost_estimate=pl.CostEstimate(flops=flops, bytes_accessed=1 << 20, transcendentals=0),
        )(*operands)

    own_half = context.shape[0] // 2
    held = lax.dynamic_slice_in_dim(context, core * own_half, own_half, 0)[None]
    targets_swapped = None
    mask = 1
    while mask < seq_count:
        other = swap(held, mask)
        if targets_swapped is None:
            targets_swapped = swap(targets, core_mask)
            grad_swapped = swap(grad_out, core_mask)
        held = jnp.concatenate([held, other], axis=0)
        mask *= 2
    other = swap(held, core_mask)

    product = 2 * half_width * rows * width
    attention = 8 * half_width * rows * context_rows
    group_width = GROUP * head_size
    groups = half_width // group_width
    (queries,) = call(
        partial(query_kernel, block),
        [place, w_query, targets, targets_swapped],
        [((half_width, rows), BF16)],
        product,
        [
            pltpu.VMEM((query_rows, width), BF16),
            pltpu.VMEM((high_count, width, block), BF16),
            pltpu.SemaphoreType.DMA((high_count + 1,)),
        ],
        (1, 2),
    )
    (grads,) = call(
        partial(grad_kernel, block),
        [place, w_out, grad_out, grad_swapped],
        [((half_width, rows), BF16)],
        product,
        [
            pltpu.VMEM((query_rows, width), BF16),
            pltpu.VMEM((high_count, block, width), BF16),
            pltpu.SemaphoreType.DMA((high_count + 1,)),
        ],
        (1, 2),
    )
    (wkv,) = call(
        partial(fetch_kernel, block, group_width),
        [place, w_key, w_value],
        [((groups, width, 2 * group_width), BF16)],
        product,
        [pltpu.SemaphoreType.DMA((2 * groups,))],
        (1, 2),
    )

    view_rows = query_rows * device_count // TVIEWS
    context_view = context_rows // CVIEWS
    firsts = jnp.stack([me, me ^ core_mask]) * query_rows // view_rows
    view_hot = firsts[:, None] == jnp.arange(TVIEWS)
    seen = jnp.sum(jnp.where(view_hot[:, :, None], visible[None], 0), axis=1)
    key_hot = jnp.arange(context_rows)[:, None] // context_view == jnp.arange(CVIEWS)
    seen = jnp.sum(jnp.where(key_hot[None], seen[:, None, :], 0), axis=2)
    bias = jnp.where(seen == 1, 0.0, -1e30).astype(BF16)
    bias = jnp.concatenate([bias, jnp.zeros((14, context_rows), BF16)], axis=0)

    key_values, probs, row_dots, wo_term = call(
        partial(attend_kernel, head_size, score_scale),
        [place, held, other, wkv, queries, grads, bias, grad_out, grad_swapped],
        [
            ((2, half_width, context_rows), BF16),
            ((half_heads, context_rows, rows), BF16),
            ((half_heads, rows), F32),
            ((half_width, width), BF16),
        ],
        product + attention,
        [
            pltpu.VMEM((context_rows, width), BF16),
            pltpu.VMEM((half_width, rows), BF16),
            pltpu.VMEM((2, query_rows, width), BF16),
            pltpu.SemaphoreType.DMA((2,)),
        ],
        (7, 8),
    )

    high_masks = []
    mask = core_mask * high_count
    while mask > core_mask:
        high_masks.append(mask)
        mask //= 2
    seq_masks = []
    mask = seq_count // 2
    while mask >= 1:
        seq_masks.append(mask)
        mask //= 2
    all_masks = high_masks + seq_masks
    high_bits = [2] * len(high_masks)
    seq_bits = [2] * len(seq_masks)
    order = [high_masks[-1], seq_masks[-1]] + seq_masks[-2::-1] + high_masks[:-1]
    stages = [tuple(order[at : at + 2]) for at in range(0, len(order), 2)]

    def exchange(array, masks, stage, last=False):
        def piece(flips):
            part = array
            for mask, flip in sorted(zip(stage, flips), key=lambda one: -masks.index(one[0])):
                at = (bit_of(mask) + flip) % 2
                part = lax.dynamic_index_in_dim(part, at, masks.index(mask), keepdims=False)
            return part

        moved = []
        for way in range(1, 2 ** len(stage)):
            flips = [way >> at & 1 for at in range(len(stage))]
            target = sum(mask for mask, flip in zip(stage, flips) if flip)
            moved.append(swap(piece(flips), target))
        total = piece([0] * len(stage)).astype(F32)
        for one in moved:
            total = total + one.astype(F32)
        left = [mask for mask in masks if mask not in stage]
        return (total if last else total.astype(BF16)), left

    def exchange_rest(array, masks):
        for at, stage in enumerate(stages[1:]):
            array, masks = exchange(array, masks, stage, at == len(stages) - 2)
        return array

    out_rows = width // device_count
    ctx_out = context_rows // device_count

    wo_split = wo_term.reshape(*high_bits, *seq_bits, out_rows, width)
    wo_part, left_masks = exchange(wo_split, all_masks, stages[0])
    grad_wo = exchange_rest(wo_part, left_masks)

    query_own, query_partner, ctx_kept, ctx_sent = call(
        partial(back_kernel, head_size, score_scale),
        [place, wkv, queries, grads, key_values, probs, row_dots],
        [
            ((half_width, query_rows), BF16),
            ((half_width, query_rows), BF16),
            ((high_count, seq_count * ctx_out, width), F32),
            ((high_count, seq_count * ctx_out, width), BF16),
        ],
        product // 2 + attention,
        scratch=[pltpu.VMEM((context_rows, width), F32)],
    )
    ctx_moved = swap(ctx_sent, core_mask)
    (wq_term,) = call(
        weight_kernel,
        [query_own, query_partner, targets, targets_swapped],
        [((width, half_width), BF16)],
        product,
    )
    ctx_pair = (ctx_kept + ctx_moved.astype(F32)).astype(BF16)
    ctx_pair = ctx_pair.reshape(*high_bits, *seq_bits, ctx_out, width)
    wq_split = wq_term.reshape(high_count, 2, seq_count, out_rows, half_width)
    tail = [wq_split[:, which].reshape(*high_bits, *seq_bits, out_rows, half_width) for which in (0, 1)]
    tail += [ctx_pair[..., :half_width], ctx_pair[..., half_width:]]
    tail, _ = exchange(jnp.concatenate(tail, axis=-2), all_masks, stages[0])
    tail = exchange_rest(tail, left_masks)

    wq_sums = tail[: 2 * out_rows].reshape(2, out_rows, half_width)
    sent = lax.dynamic_index_in_dim(wq_sums, 1 - core, 0, keepdims=False)
    mine = lax.dynamic_index_in_dim(wq_sums, core, 0, keepdims=False)
    theirs = swap(sent, core_mask)
    pieces = []
    for at in range(0, half_width, block):
        pieces.append(jnp.where(core == 0, mine[:, at : at + block], theirs[:, at : at + block]))
        pieces.append(jnp.where(core == 0, theirs[:, at : at + block], mine[:, at : at + block]))
    grad_wq = jnp.concatenate(pieces, axis=1)
    ctx_sums = tail[2 * out_rows :]
    d_context = jnp.concatenate([ctx_sums[:ctx_out], ctx_sums[ctx_out:]], axis=1).astype(BF16)

    returned = swap(query_partner, core_mask)
    (d_targets,) = call(
        partial(targets_kernel, block),
        [place, query_own, returned, w_query],
        [((query_rows, width), BF16)],
        product,
    )
    return (d_targets, d_context, grad_wq, grad_wo)


def solution(mesh):
    in_specs = (
        P(AXES, None),
        P("seq", None),
        P(),
        P(),
        P(),
        P(),
        P(),
        P(AXES, None),
    )
    out_specs = (P(AXES, None), P(AXES, None), P(AXES, None), P(AXES, None))

    return jax.shard_map(
        on_device, mesh=mesh, in_specs=in_specs, out_specs=out_specs, check_vma=False
    )
```

```python
from functools import partial

import jax
import jax.numpy as jnp
from jax import lax
from jax.experimental import pallas as pl
from jax.experimental.pallas import tpu as pltpu
from jax.sharding import PartitionSpec as P


HEADS = 16
TVIEWS = 8
CVIEWS = 16
AXES = ("grp", "seq")
GROUP = 2

F32 = jnp.float32
BF16 = jnp.bfloat16


def dot(left, right, dims):
    return lax.dot_general(left, right, (dims, ((), ())), preferred_element_type=F32)


def owned(place_ref, at, size, block):
    return pl.ds(pl.multiple_of((2 * (at // block) + place_ref[0]) * block + at % block, size), size)


def query_kernel(block, place_ref, weight_ref, own_ref, partner_ref, out_ref, tokens, weights, sems):
    rows = partner_ref.shape[0]
    count = weights.shape[0]
    copies = []
    for at in range(count):
        part = owned(place_ref, at * block, block, block)
        copies.append(pltpu.make_async_copy(weight_ref.at[:, part], weights.at[at], sems.at[at]))
    copies.append(pltpu.make_async_copy(own_ref, tokens, sems.at[count]))
    for one in copies:
        one.start()
    for side, source in enumerate((partner_ref, tokens)):
        if side == 1:
            copies[count].wait()
        for at in range(count):
            if side == 0:
                copies[at].wait()
            term = dot(source[...], weights[at], ((1,), (0,))).astype(BF16).T
            out_ref[pl.ds(at * block, block), pl.ds((1 - side) * rows, rows)] = term


def grad_kernel(block, place_ref, weight_ref, own_ref, partner_ref, out_ref, tokens, weights, sems):
    rows = partner_ref.shape[0]
    count = weights.shape[0]
    copies = []
    for at in range(count):
        part = owned(place_ref, at * block, block, block)
        copies.append(pltpu.make_async_copy(weight_ref.at[part, :], weights.at[at], sems.at[at]))
    copies.append(pltpu.make_async_copy(own_ref, tokens, sems.at[count]))
    for one in copies:
        one.start()
    for side, source in enumerate((partner_ref, tokens)):
        if side == 1:
            copies[count].wait()
        for at in range(count):
            if side == 0:
                copies[at].wait()
            term = dot(weights[at], source[...], ((1,), (1,))).astype(BF16)
            out_ref[pl.ds(at * block, block), pl.ds((1 - side) * rows, rows)] = term


def fetch_kernel(block, group, place_ref, wk_ref, wv_ref, wkv_ref, sems):
    copies = []
    for at in range(wkv_ref.shape[0]):
        part = owned(place_ref, at * group, group, block)
        for which, source in enumerate((wk_ref, wv_ref)):
            target = wkv_ref.at[at, :, pl.ds(which * group, group)]
            copies.append(
                pltpu.make_async_copy(source.at[:, part], target, sems.at[2 * at + which])
            )
            copies[-1].start()
    for one in copies:
        one.wait()


def attend_kernel(
    size,
    scale,
    place_ref,
    mine_ref,
    other_ref,
    wkv_ref,
    q_ref,
    g_ref,
    bias_ref,
    own_ref,
    partner_ref,
    kv_ref,
    probs_ref,
    row_dot_ref,
    wo_ref,
    context_ref,
    att_ref,
    tokens,
    sems,
):
    half_width, rows = q_ref.shape
    block_rows = rows // 2
    width = GROUP * size
    moves = []
    for side, source in enumerate((own_ref, partner_ref)):
        moves.append(pltpu.make_async_copy(source, tokens.at[side], sems.at[side]))
        moves[-1].start()
    shards, half_rows = mine_ref.shape[:2]
    for at in range(shards):
        first = lax.bitwise_xor(place_ref[1], at) * 2 * half_rows
        mine = pl.multiple_of(first + place_ref[0] * half_rows, half_rows)
        other = pl.multiple_of(first + (1 - place_ref[0]) * half_rows, half_rows)
        context_ref[pl.ds(mine, half_rows), :] = mine_ref[at]
        context_ref[pl.ds(other, half_rows), :] = other_ref[at]
    context = context_ref[...]
    bias = bias_ref[...]
    lane = lax.broadcasted_iota(jnp.int32, (16, rows), 1)
    line = lax.broadcasted_iota(jnp.int32, (16, rows), 0)
    marks = jnp.where(lane // block_rows == line, 1.0, 0.0).astype(BF16)

    def keys_values(at):
        step = at // width
        both = dot(context, wkv_ref[step], ((1,), (0,))).astype(BF16)
        key_part = (both[:, :width].astype(F32) * scale).astype(BF16)
        kv_ref[0, pl.ds(at, width), :] = key_part.T
        kv_ref[1, pl.ds(at, width), :] = both[:, width:].T

    def score(first):
        part = pl.ds(first, size)
        key_rows = jnp.concatenate([kv_ref[0, part, :], bias], axis=0)
        query_rows = jnp.concatenate([q_ref[part, :], marks], axis=0)
        return dot(key_rows.T, query_rows, ((1,), (0,)))

    keys_values(0)
    following = score(0)
    for at in range(0, half_width, width):
        if at + width < half_width:
            keys_values(at + width)
        for first in range(at, at + width, size):
            part = pl.ds(first, size)
            scores = following
            if first + size < half_width:
                following = score(first + size)
            row_max = jnp.max(scores, axis=0, keepdims=True)
            unnormed = jnp.exp(scores - row_max)
            row_sum = jnp.sum(unnormed, axis=0, keepdims=True)
            probs = (unnormed * (1.0 / row_sum)).astype(BF16)
            probs_ref[first // size] = probs
            attended = dot(kv_ref[1, part, :], probs, ((1,), (0,))).astype(BF16)
            att_ref[part, :] = attended
            row_dot = attended.astype(F32) * g_ref[part, :].astype(F32)
            row_dot_ref[pl.ds(first // size, 1), :] = jnp.sum(row_dot, axis=0, keepdims=True)
        if (at // width) % 2 == 1:
            if at == width:
                for move in moves:
                    move.wait()
            part = pl.ds(at - width, 2 * width)
            total = dot(att_ref[part, :block_rows], tokens[0], ((1,), (0,)))
            total += dot(att_ref[part, block_rows:], tokens[1], ((1,), (0,)))
            wo_ref[part, :] = total.astype(BF16)


def back_kernel(
    size,
    scale,
    place_ref,
    wkv_ref,
    q_ref,
    g_ref,
    kv_ref,
    probs_ref,
    row_dot_ref,
    qg_own_ref,
    qg_partner_ref,
    kept_ref,
    sent_ref,
    sum_ref,
):
    half_width = q_ref.shape[0]
    block_rows = qg_own_ref.shape[1]
    width = GROUP * size

    def score_grads(first):
        part = pl.ds(first, size)
        return dot(kv_ref[1, part, :].T, g_ref[part, :], ((1,), (0,)))

    following = score_grads(0)
    for at in range(0, half_width, width):
        key_parts, value_parts = [], []
        for first in range(at, at + width, size):
            part = pl.ds(first, size)
            grad_scores = following
            if first + size < half_width:
                following = score_grads(first + size)
            probs = probs_ref[first // size]
            value_parts.append(dot(g_ref[part, :], probs, ((1,), (1,))))
            row_dot = row_dot_ref[pl.ds(first // size, 1), :]
            logits = (probs.astype(F32) * (grad_scores - row_dot)).astype(BF16)
            query_grad = dot(kv_ref[0, part, :], logits, ((1,), (0,))).astype(BF16)
            qg_own_ref[part, :] = query_grad[:, :block_rows]
            qg_partner_ref[part, :] = query_grad[:, block_rows:]
            key_parts.append(dot(q_ref[part, :], logits, ((1,), (1,))) * scale)
        grads = jnp.concatenate(key_parts + value_parts, axis=0).astype(BF16).T
        term = dot(grads, wkv_ref[at // width], ((1,), (1,)))
        if at == 0:
            sum_ref[...] = term
        else:
            sum_ref[...] += term
    out_block = kept_ref.shape[1]
    for high in range(kept_ref.shape[0]):
        kept = pl.multiple_of((2 * high + place_ref[0]) * out_block, out_block)
        sent = pl.multiple_of((2 * high + 1 - place_ref[0]) * out_block, out_block)
        kept_ref[high] = sum_ref[pl.ds(kept, out_block), :]
        sent_ref[high] = sum_ref[pl.ds(sent, out_block), :].astype(BF16)


def weight_kernel(at, qg_own_ref, qg_partner_ref, own_ref, partner_ref, out_ref):
    part = pl.ds(at, out_ref.shape[1])
    total = dot(qg_own_ref[part, :], own_ref[...], ((1,), (0,)))
    total += dot(qg_partner_ref[part, :], partner_ref[...], ((1,), (0,)))
    out_ref[...] = total.astype(BF16).T


def targets_kernel(block, place_ref, mine_ref, theirs_ref, weight_ref, out_ref, weights, sems):
    other_ref = [1 - place_ref[0]]
    copies, sources = [], []
    for at in range(0, mine_ref.shape[0], block):
        for source, core in ((mine_ref, place_ref), (theirs_ref, other_ref)):
            index = len(copies)
            columns = weight_ref.at[:, owned(core, at, block, block)]
            copies.append(pltpu.make_async_copy(columns, weights.at[index], sems.at[index]))
            copies[-1].start()
            sources.append(source[pl.ds(at, block), :])
    total = None
    for index, source in enumerate(sources):
        copies[index].wait()
        term = dot(source.T, weights[index], ((1,), (1,)))
        total = term if total is None else total + term
    out_ref[...] = total.astype(BF16)


def on_device(targets, context, w_query, w_key, w_value, w_out, visible, grad_out):
    query_rows, width = targets.shape
    head_size = width // HEADS
    score_scale = head_size ** (-0.5)
    grp_count = lax.axis_size("grp")
    seq_count = lax.axis_size("seq")
    device_count = grp_count * seq_count
    grp = lax.axis_index("grp")
    seq = lax.axis_index("seq")
    me = grp * seq_count + seq
    core = grp % 2
    core_mask = seq_count
    high_count = grp_count // 2
    half_width = width // 2
    half_heads = HEADS // 2
    block = width // grp_count
    context_rows = context.shape[0] * seq_count
    rows = 2 * query_rows
    place = jnp.stack([core, seq]).astype(jnp.int32)
    limit = (14 << 20) + 6 * 4 * context_rows * rows

    def swap(array, mask):
        return lax.ppermute(array, AXES, [(i, i ^ mask) for i in range(device_count)])

    def bit_of(mask):
        return (me // mask) % 2

    def call(kernel, operands, outs, flops, scratch=(), fetched=()):
        in_vmem = pl.BlockSpec(memory_space=pltpu.VMEM)
        scalar = pl.BlockSpec(memory_space=pltpu.SMEM)
        anywhere = pl.BlockSpec(memory_space=pltpu.HBM)
        specs = [scalar if one is place else in_vmem for one in operands]
        operands = list(operands)
        for at in fetched:
            specs[at] = anywhere
            operands[at] = pltpu.with_memory_space_constraint(operands[at], pltpu.HBM)
        return pl.pallas_call(
            kernel,
            in_specs=specs,
            out_specs=[in_vmem] * len(outs),
            out_shape=[jax.ShapeDtypeStruct(shape, kind) for shape, kind in outs],
            scratch_shapes=scratch,
            compiler_params=pltpu.CompilerParams(vmem_limit_bytes=limit),
            cost_estimate=pl.CostEstimate(flops=flops, bytes_accessed=1 << 20, transcendentals=0),
        )(*operands)

    own_half = context.shape[0] // 2
    held = lax.dynamic_slice_in_dim(context, core * own_half, own_half, 0)[None]
    targets_swapped = None
    mask = 1
    while mask < seq_count:
        other = swap(held, mask)
        if targets_swapped is None:
            targets_swapped = swap(targets, core_mask)
            grad_swapped = swap(grad_out, core_mask)
        held = jnp.concatenate([held, other], axis=0)
        mask *= 2
    other = swap(held, core_mask)

    product = 2 * half_width * rows * width
    attention = 8 * half_width * rows * context_rows
    group_width = GROUP * head_size
    groups = half_width // group_width
    (queries,) = call(
        partial(query_kernel, block),
        [place, w_query, targets, targets_swapped],
        [((half_width, rows), BF16)],
        product,
        [
            pltpu.VMEM((query_rows, width), BF16),
            pltpu.VMEM((high_count, width, block), BF16),
            pltpu.SemaphoreType.DMA((high_count + 1,)),
        ],
        (1, 2),
    )
    (grads,) = call(
        partial(grad_kernel, block),
        [place, w_out, grad_out, grad_swapped],
        [((half_width, rows), BF16)],
        product,
        [
            pltpu.VMEM((query_rows, width), BF16),
            pltpu.VMEM((high_count, block, width), BF16),
            pltpu.SemaphoreType.DMA((high_count + 1,)),
        ],
        (1, 2),
    )
    (wkv,) = call(
        partial(fetch_kernel, block, group_width),
        [place, w_key, w_value],
        [((groups, width, 2 * group_width), BF16)],
        product,
        [pltpu.SemaphoreType.DMA((2 * groups,))],
        (1, 2),
    )

    view_rows = query_rows * device_count // TVIEWS
    context_view = context_rows // CVIEWS
    firsts = jnp.stack([me, me ^ core_mask]) * query_rows // view_rows
    view_hot = firsts[:, None] == jnp.arange(TVIEWS)
    seen = jnp.sum(jnp.where(view_hot[:, :, None], visible[None], 0), axis=1)
    key_hot = jnp.arange(context_rows)[:, None] // context_view == jnp.arange(CVIEWS)
    seen = jnp.sum(jnp.where(key_hot[None], seen[:, None, :], 0), axis=2)
    bias = jnp.where(seen == 1, 0.0, -1e30).astype(BF16)
    bias = jnp.concatenate([bias, jnp.zeros((14, context_rows), BF16)], axis=0)

    key_values, probs, row_dots, wo_term = call(
        partial(attend_kernel, head_size, score_scale),
        [place, held, other, wkv, queries, grads, bias, grad_out, grad_swapped],
        [
            ((2, half_width, context_rows), BF16),
            ((half_heads, context_rows, rows), BF16),
            ((half_heads, rows), F32),
            ((half_width, width), BF16),
        ],
        product + attention,
        [
            pltpu.VMEM((context_rows, width), BF16),
            pltpu.VMEM((half_width, rows), BF16),
            pltpu.VMEM((2, query_rows, width), BF16),
            pltpu.SemaphoreType.DMA((2,)),
        ],
        (7, 8),
    )

    high_masks = []
    mask = core_mask * high_count
    while mask > core_mask:
        high_masks.append(mask)
        mask //= 2
    seq_masks = []
    mask = seq_count // 2
    while mask >= 1:
        seq_masks.append(mask)
        mask //= 2
    all_masks = high_masks + seq_masks
    high_bits = [2] * len(high_masks)
    seq_bits = [2] * len(seq_masks)
    order = [high_masks[-1], seq_masks[-1]] + seq_masks[-2::-1] + high_masks[:-1]
    stages = [tuple(order[at : at + 2]) for at in range(0, len(order), 2)]

    def exchange(array, masks, stage, last=False):
        def piece(flips):
            part = array
            for mask, flip in sorted(zip(stage, flips), key=lambda one: -masks.index(one[0])):
                at = (bit_of(mask) + flip) % 2
                part = lax.dynamic_index_in_dim(part, at, masks.index(mask), keepdims=False)
            return part

        moved = []
        for way in range(1, 2 ** len(stage)):
            flips = [way >> at & 1 for at in range(len(stage))]
            target = sum(mask for mask, flip in zip(stage, flips) if flip)
            moved.append(swap(piece(flips), target))
        total = piece([0] * len(stage)).astype(F32)
        for one in moved:
            total = total + one.astype(F32)
        total = total if last else total.astype(BF16)
        left = [mask for mask in masks if mask not in stage]
        return total, left

    def exchange_rest(array, masks):
        for at, stage in enumerate(stages[1:]):
            array, masks = exchange(array, masks, stage, at == len(stages) - 2)
        return array

    out_rows = width // device_count
    ctx_out = context_rows // device_count

    wo_split = wo_term.reshape(*high_bits, *seq_bits, out_rows, width)
    wo_part, left_masks = exchange(wo_split, all_masks, stages[0])

    query_own, query_partner, ctx_kept, ctx_sent = call(
        partial(back_kernel, head_size, score_scale),
        [place, wkv, queries, grads, key_values, probs, row_dots],
        [
            ((half_width, query_rows), BF16),
            ((half_width, query_rows), BF16),
            ((high_count, seq_count * ctx_out, width), F32),
            ((high_count, seq_count * ctx_out, width), BF16),
        ],
        product // 2 + attention,
        scratch=[pltpu.VMEM((context_rows, width), F32)],
    )
    ctx_moved = swap(ctx_sent, core_mask)

    def stacked(array):
        return [array[..., at : at + block] for at in range(0, array.shape[-1], block)]

    parts = []
    for part in range(high_count):
        (wq_term,) = call(
            partial(weight_kernel, part * block),
            [query_own, query_partner, targets, targets_swapped],
            [((width, block), BF16)],
            product // high_count,
        )
        wq_split = wq_term.reshape(high_count, 2, seq_count, out_rows, block)
        pieces = [
            wq_split[:, which].reshape(*high_bits, *seq_bits, out_rows, block) for which in (0, 1)
        ]
        if part == 0:
            ctx_pair = (ctx_kept + ctx_moved.astype(F32)).astype(BF16)
            pieces += stacked(ctx_pair.reshape(*high_bits, *seq_bits, ctx_out, width))
        moved, _ = exchange(jnp.concatenate(pieces, axis=-2), all_masks, stages[0])
        parts.append(exchange_rest(moved, left_masks))

    first = parts[0]
    edges = [2 * out_rows, 2 * out_rows + grp_count * ctx_out]
    wq_sums = jnp.stack([one[: edges[0]].reshape(2, out_rows, block) for one in parts])
    ctx_sums = first[edges[0] : edges[1]].reshape(grp_count, ctx_out, block)
    d_context = jnp.concatenate(list(ctx_sums), axis=1).astype(BF16)
    grad_wo = exchange_rest(wo_part, left_masks)
    sent = lax.dynamic_index_in_dim(wq_sums, 1 - core, 1, keepdims=False)
    mine = lax.dynamic_index_in_dim(wq_sums, core, 1, keepdims=False)
    theirs = swap(sent, core_mask)
    pieces = []
    for part in range(high_count):
        pieces.append(jnp.where(core == 0, mine[part], theirs[part]))
        pieces.append(jnp.where(core == 0, theirs[part], mine[part]))
    grad_wq = jnp.concatenate(pieces, axis=1)

    returned = swap(query_partner, core_mask)
    (d_targets,) = call(
        partial(targets_kernel, block),
        [place, query_own, returned, w_query],
        [((query_rows, width), BF16)],
        product,
        [pltpu.VMEM((grp_count, width, block), BF16), pltpu.SemaphoreType.DMA((grp_count,))],
        (3,),
    )
    return (d_targets, d_context, grad_wq, grad_wo)


def solution(mesh):
    in_specs = (
        P(AXES, None),
        P("seq", None),
        P(),
        P(),
        P(),
        P(),
        P(),
        P(AXES, None),
    )
    out_specs = (P(AXES, None), P(AXES, None), P(AXES, None), P(AXES, None))

    return jax.shard_map(
        on_device, mesh=mesh, in_specs=in_specs, out_specs=out_specs, check_vma=False
    )
```

```python
from functools import partial

import jax
import jax.numpy as jnp
from jax import lax
from jax.experimental import pallas as pl
from jax.experimental.pallas import tpu as pltpu
from jax.sharding import PartitionSpec as P


HEADS = 16
TVIEWS = 8
CVIEWS = 16
AXES = ("grp", "seq")
GROUP = 2

F32 = jnp.float32
BF16 = jnp.bfloat16


def dot(left, right, dims):
    return lax.dot_general(left, right, (dims, ((), ())), preferred_element_type=F32)


def owned(place_ref, at, size, block):
    return pl.ds(pl.multiple_of((2 * (at // block) + place_ref[0]) * block + at % block, size), size)


def query_kernel(block, place_ref, weight_ref, own_ref, partner_ref, out_ref, tokens, weights, sems):
    rows = partner_ref.shape[0]
    count = weights.shape[0]
    copies = []
    for at in range(count):
        part = owned(place_ref, at * block, block, block)
        copies.append(pltpu.make_async_copy(weight_ref.at[:, part], weights.at[at], sems.at[at]))
    copies.append(pltpu.make_async_copy(own_ref, tokens, sems.at[count]))
    for one in copies:
        one.start()
    for side, source in enumerate((partner_ref, tokens)):
        if side == 1:
            copies[count].wait()
        for at in range(count):
            if side == 0:
                copies[at].wait()
            term = dot(source[...], weights[at], ((1,), (0,))).astype(BF16).T
            out_ref[pl.ds(at * block, block), pl.ds((1 - side) * rows, rows)] = term


def grad_kernel(block, place_ref, weight_ref, own_ref, partner_ref, out_ref, tokens, weights, sems):
    rows = partner_ref.shape[0]
    count = weights.shape[0]
    copies = []
    for at in range(count):
        part = owned(place_ref, at * block, block, block)
        copies.append(pltpu.make_async_copy(weight_ref.at[part, :], weights.at[at], sems.at[at]))
    copies.append(pltpu.make_async_copy(own_ref, tokens, sems.at[count]))
    for one in copies:
        one.start()
    for side, source in enumerate((partner_ref, tokens)):
        if side == 1:
            copies[count].wait()
        for at in range(count):
            if side == 0:
                copies[at].wait()
            term = dot(weights[at], source[...], ((1,), (1,))).astype(BF16)
            out_ref[pl.ds(at * block, block), pl.ds((1 - side) * rows, rows)] = term


def fetch_kernel(block, group, place_ref, wk_ref, wv_ref, wkv_ref, sems):
    copies = []
    for at in range(wkv_ref.shape[0]):
        part = owned(place_ref, at * group, group, block)
        for which, source in enumerate((wk_ref, wv_ref)):
            target = wkv_ref.at[at, :, pl.ds(which * group, group)]
            copies.append(
                pltpu.make_async_copy(source.at[:, part], target, sems.at[2 * at + which])
            )
            copies[-1].start()
    for one in copies:
        one.wait()


def attend_kernel(
    size,
    scale,
    place_ref,
    mine_ref,
    other_ref,
    wkv_ref,
    q_ref,
    g_ref,
    bias_ref,
    own_ref,
    partner_ref,
    kv_ref,
    probs_ref,
    row_dot_ref,
    wo_ref,
    context_ref,
    att_ref,
    tokens,
    sems,
):
    half_width, rows = q_ref.shape
    block_rows = rows // 2
    width = GROUP * size
    moves = []
    for side, source in enumerate((own_ref, partner_ref)):
        moves.append(pltpu.make_async_copy(source, tokens.at[side], sems.at[side]))
        moves[-1].start()
    shards, half_rows = mine_ref.shape[:2]
    for at in range(shards):
        first = lax.bitwise_xor(place_ref[1], at) * 2 * half_rows
        mine = pl.multiple_of(first + place_ref[0] * half_rows, half_rows)
        other = pl.multiple_of(first + (1 - place_ref[0]) * half_rows, half_rows)
        context_ref[pl.ds(mine, half_rows), :] = mine_ref[at]
        context_ref[pl.ds(other, half_rows), :] = other_ref[at]
    context = context_ref[...]
    bias = bias_ref[...]
    lane = lax.broadcasted_iota(jnp.int32, (16, rows), 1)
    line = lax.broadcasted_iota(jnp.int32, (16, rows), 0)
    marks = jnp.where(lane // block_rows == line, 1.0, 0.0).astype(BF16)

    def keys_values(at):
        step = at // width
        both = dot(context, wkv_ref[step], ((1,), (0,))).astype(BF16)
        key_part = (both[:, :width].astype(F32) * scale).astype(BF16)
        kv_ref[0, pl.ds(at, width), :] = key_part.T
        kv_ref[1, pl.ds(at, width), :] = both[:, width:].T

    def score(first):
        part = pl.ds(first, size)
        key_rows = jnp.concatenate([kv_ref[0, part, :], bias], axis=0)
        query_rows = jnp.concatenate([q_ref[part, :], marks], axis=0)
        return dot(key_rows.T, query_rows, ((1,), (0,)))

    keys_values(0)
    following = score(0)
    for at in range(0, half_width, width):
        if at + width < half_width:
            keys_values(at + width)
        for first in range(at, at + width, size):
            part = pl.ds(first, size)
            scores = following
            if first + size < half_width:
                following = score(first + size)
            row_max = jnp.max(scores, axis=0, keepdims=True)
            unnormed = jnp.exp(scores - row_max)
            row_sum = jnp.sum(unnormed, axis=0, keepdims=True)
            probs = (unnormed * (1.0 / row_sum)).astype(BF16)
            probs_ref[first // size] = probs
            attended = dot(kv_ref[1, part, :], probs, ((1,), (0,))).astype(BF16)
            att_ref[part, :] = attended
            row_dot = attended.astype(F32) * g_ref[part, :].astype(F32)
            row_dot_ref[pl.ds(first // size, 1), :] = jnp.sum(row_dot, axis=0, keepdims=True)
        if (at // width) % 2 == 1:
            if at == width:
                for move in moves:
                    move.wait()
            part = pl.ds(at - width, 2 * width)
            total = dot(att_ref[part, :block_rows], tokens[0], ((1,), (0,)))
            total += dot(att_ref[part, block_rows:], tokens[1], ((1,), (0,)))
            wo_ref[part, :] = total.astype(BF16)


def back_kernel(
    size,
    scale,
    place_ref,
    wkv_ref,
    q_ref,
    g_ref,
    kv_ref,
    probs_ref,
    row_dot_ref,
    qg_own_ref,
    qg_partner_ref,
    kept_ref,
    sent_ref,
    sum_ref,
):
    half_width = q_ref.shape[0]
    block_rows = qg_own_ref.shape[1]
    width = GROUP * size

    def score_grads(first):
        part = pl.ds(first, size)
        return dot(kv_ref[1, part, :].T, g_ref[part, :], ((1,), (0,)))

    following = score_grads(0)
    for at in range(0, half_width, width):
        key_parts, value_parts = [], []
        for first in range(at, at + width, size):
            part = pl.ds(first, size)
            grad_scores = following
            if first + size < half_width:
                following = score_grads(first + size)
            probs = probs_ref[first // size]
            value_parts.append(dot(g_ref[part, :], probs, ((1,), (1,))))
            row_dot = row_dot_ref[pl.ds(first // size, 1), :]
            logits = (probs.astype(F32) * (grad_scores - row_dot)).astype(BF16)
            query_grad = dot(kv_ref[0, part, :], logits, ((1,), (0,))).astype(BF16)
            qg_own_ref[part, :] = query_grad[:, :block_rows]
            qg_partner_ref[part, :] = query_grad[:, block_rows:]
            key_parts.append(dot(q_ref[part, :], logits, ((1,), (1,))) * scale)
        grads = jnp.concatenate(key_parts + value_parts, axis=0).astype(BF16).T
        term = dot(grads, wkv_ref[at // width], ((1,), (1,)))
        if at == 0:
            sum_ref[...] = term
        else:
            sum_ref[...] += term
    out_block = kept_ref.shape[1]
    for high in range(kept_ref.shape[0]):
        kept = pl.multiple_of((2 * high + place_ref[0]) * out_block, out_block)
        sent = pl.multiple_of((2 * high + 1 - place_ref[0]) * out_block, out_block)
        kept_ref[high] = sum_ref[pl.ds(kept, out_block), :]
        sent_ref[high] = sum_ref[pl.ds(sent, out_block), :].astype(BF16)


def weight_kernel(at, qg_own_ref, qg_partner_ref, own_ref, partner_ref, out_ref):
    part = pl.ds(at, out_ref.shape[1])
    total = dot(qg_own_ref[part, :], own_ref[...], ((1,), (0,)))
    total += dot(qg_partner_ref[part, :], partner_ref[...], ((1,), (0,)))
    out_ref[...] = total.astype(BF16).T


def targets_kernel(block, place_ref, mine_ref, theirs_ref, weight_ref, out_ref):
    other_ref = [1 - place_ref[0]]
    total = None
    for at in range(0, mine_ref.shape[0], block):
        part = pl.ds(at, block)
        for source, core in ((mine_ref, place_ref), (theirs_ref, other_ref)):
            weight = weight_ref[:, owned(core, at, block, block)]
            term = dot(source[part, :].T, weight, ((1,), (1,)))
            total = term if total is None else total + term
    out_ref[...] = total.astype(BF16)


def on_device(targets, context, w_query, w_key, w_value, w_out, visible, grad_out):
    query_rows, width = targets.shape
    head_size = width // HEADS
    score_scale = head_size ** (-0.5)
    grp_count = lax.axis_size("grp")
    seq_count = lax.axis_size("seq")
    device_count = grp_count * seq_count
    grp = lax.axis_index("grp")
    seq = lax.axis_index("seq")
    me = grp * seq_count + seq
    core = grp % 2
    core_mask = seq_count
    high_count = grp_count // 2
    half_width = width // 2
    half_heads = HEADS // 2
    block = width // grp_count
    context_rows = context.shape[0] * seq_count
    rows = 2 * query_rows
    place = jnp.stack([core, seq]).astype(jnp.int32)
    limit = (14 << 20) + 6 * 4 * context_rows * rows

    def swap(array, mask):
        return lax.ppermute(array, AXES, [(i, i ^ mask) for i in range(device_count)])

    def bit_of(mask):
        return (me // mask) % 2

    def call(kernel, operands, outs, flops, scratch=(), fetched=()):
        in_vmem = pl.BlockSpec(memory_space=pltpu.VMEM)
        scalar = pl.BlockSpec(memory_space=pltpu.SMEM)
        anywhere = pl.BlockSpec(memory_space=pltpu.HBM)
        specs = [scalar if one is place else in_vmem for one in operands]
        operands = list(operands)
        for at in fetched:
            specs[at] = anywhere
            operands[at] = pltpu.with_memory_space_constraint(operands[at], pltpu.HBM)
        return pl.pallas_call(
            kernel,
            in_specs=specs,
            out_specs=[in_vmem] * len(outs),
            out_shape=[jax.ShapeDtypeStruct(shape, kind) for shape, kind in outs],
            scratch_shapes=scratch,
            compiler_params=pltpu.CompilerParams(vmem_limit_bytes=limit),
            cost_estimate=pl.CostEstimate(flops=flops, bytes_accessed=1 << 20, transcendentals=0),
        )(*operands)

    own_half = context.shape[0] // 2
    held = lax.dynamic_slice_in_dim(context, core * own_half, own_half, 0)[None]
    targets_swapped = None
    mask = 1
    while mask < seq_count:
        other = swap(held, mask)
        if targets_swapped is None:
            targets_swapped = swap(targets, core_mask)
            grad_swapped = swap(grad_out, core_mask)
        held = jnp.concatenate([held, other], axis=0)
        mask *= 2
    other = swap(held, core_mask)

    product = 2 * half_width * rows * width
    attention = 8 * half_width * rows * context_rows
    group_width = GROUP * head_size
    groups = half_width // group_width
    (queries,) = call(
        partial(query_kernel, block),
        [place, w_query, targets, targets_swapped],
        [((half_width, rows), BF16)],
        product,
        [
            pltpu.VMEM((query_rows, width), BF16),
            pltpu.VMEM((high_count, width, block), BF16),
            pltpu.SemaphoreType.DMA((high_count + 1,)),
        ],
        (1, 2),
    )
    (grads,) = call(
        partial(grad_kernel, block),
        [place, w_out, grad_out, grad_swapped],
        [((half_width, rows), BF16)],
        product,
        [
            pltpu.VMEM((query_rows, width), BF16),
            pltpu.VMEM((high_count, block, width), BF16),
            pltpu.SemaphoreType.DMA((high_count + 1,)),
        ],
        (1, 2),
    )
    (wkv,) = call(
        partial(fetch_kernel, block, group_width),
        [place, w_key, w_value],
        [((groups, width, 2 * group_width), BF16)],
        product,
        [pltpu.SemaphoreType.DMA((2 * groups,))],
        (1, 2),
    )

    view_rows = query_rows * device_count // TVIEWS
    context_view = context_rows // CVIEWS
    firsts = jnp.stack([me, me ^ core_mask]) * query_rows // view_rows
    view_hot = firsts[:, None] == jnp.arange(TVIEWS)
    seen = jnp.sum(jnp.where(view_hot[:, :, None], visible[None], 0), axis=1)
    key_hot = jnp.arange(context_rows)[:, None] // context_view == jnp.arange(CVIEWS)
    seen = jnp.sum(jnp.where(key_hot[None], seen[:, None, :], 0), axis=2)
    bias = jnp.where(seen == 1, 0.0, -1e30).astype(BF16)
    bias = jnp.concatenate([bias, jnp.zeros((14, context_rows), BF16)], axis=0)

    key_values, probs, row_dots, wo_term = call(
        partial(attend_kernel, head_size, score_scale),
        [place, held, other, wkv, queries, grads, bias, grad_out, grad_swapped],
        [
            ((2, half_width, context_rows), BF16),
            ((half_heads, context_rows, rows), BF16),
            ((half_heads, rows), F32),
            ((half_width, width), BF16),
        ],
        product + attention,
        [
            pltpu.VMEM((context_rows, width), BF16),
            pltpu.VMEM((half_width, rows), BF16),
            pltpu.VMEM((2, query_rows, width), BF16),
            pltpu.SemaphoreType.DMA((2,)),
        ],
        (7, 8),
    )

    high_masks = []
    mask = core_mask * high_count
    while mask > core_mask:
        high_masks.append(mask)
        mask //= 2
    seq_masks = []
    mask = seq_count // 2
    while mask >= 1:
        seq_masks.append(mask)
        mask //= 2
    all_masks = high_masks + seq_masks
    high_bits = [2] * len(high_masks)
    seq_bits = [2] * len(seq_masks)
    order = [high_masks[-1], seq_masks[-1]] + seq_masks[-2::-1] + high_masks[:-1]
    stages = [tuple(order[:2])]

    def exchange(array, masks, stage, last=False):
        def piece(flips):
            part = array
            for mask, flip in sorted(zip(stage, flips), key=lambda one: -masks.index(one[0])):
                at = (bit_of(mask) + flip) % 2
                part = lax.dynamic_index_in_dim(part, at, masks.index(mask), keepdims=False)
            return part

        moved = []
        for way in range(1, 2 ** len(stage)):
            flips = [way >> at & 1 for at in range(len(stage))]
            target = sum(mask for mask, flip in zip(stage, flips) if flip)
            moved.append(swap(piece(flips), target))
        total = piece([0] * len(stage)).astype(F32)
        for one in moved:
            total = total + one.astype(F32)
        total = total if last else total.astype(BF16)
        left = [mask for mask in masks if mask not in stage]
        return total, left

    def exchange_rest(array, masks, steps):
        for at, stage in enumerate(steps):
            array, masks = exchange(array, masks, stage, at == len(steps) - 1)
        return array

    def paired(masks):
        return [tuple(masks[at : at + 2]) for at in range(0, len(masks), 2)]

    late_steps = paired(order[2:])
    early_steps = [tuple(order[3:4])] + paired(order[4:])

    out_rows = width // device_count
    ctx_out = context_rows // device_count

    wo_split = wo_term.reshape(*high_bits, *seq_bits, out_rows, width)
    wo_part, left_masks = exchange(wo_split, all_masks, stages[0])

    query_own, query_partner, ctx_kept, ctx_sent = call(
        partial(back_kernel, head_size, score_scale),
        [place, wkv, queries, grads, key_values, probs, row_dots],
        [
            ((half_width, query_rows), BF16),
            ((half_width, query_rows), BF16),
            ((high_count, seq_count * ctx_out, width), F32),
            ((high_count, seq_count * ctx_out, width), BF16),
        ],
        product // 2 + attention,
        scratch=[pltpu.VMEM((context_rows, width), F32)],
    )
    ctx_moved = swap(ctx_sent, core_mask)

    def stacked(array):
        return [array[..., at : at + block] for at in range(0, array.shape[-1], block)]

    parts = []
    for part in range(high_count):
        (wq_term,) = call(
            partial(weight_kernel, part * block),
            [query_own, query_partner, targets, targets_swapped],
            [((width, block), BF16)],
            product // high_count,
        )
        wq_split = wq_term.reshape(high_count, 2, seq_count, out_rows, block)
        pieces = [
            wq_split[:, which].reshape(*high_bits, *seq_bits, out_rows, block) for which in (0, 1)
        ]
        if part == 0:
            ctx_pair = (ctx_kept + ctx_moved.astype(F32)).astype(BF16)
            pieces += stacked(ctx_pair.reshape(*high_bits, *seq_bits, ctx_out, width))
        moved, _ = exchange(jnp.concatenate(pieces, axis=-2), all_masks, stages[0])
        if part == 0:
            moved, early_masks = exchange(moved, left_masks, order[2:3])
            wo_half, _ = exchange(wo_part, left_masks, order[2:3])
            moved = jnp.concatenate([moved] + stacked(wo_half), axis=-2)
            parts.append(exchange_rest(moved, early_masks, early_steps))
        else:
            parts.append(exchange_rest(moved, left_masks, late_steps))

    first = parts[0]
    edges = [2 * out_rows, 2 * out_rows + grp_count * ctx_out]
    wq_sums = jnp.stack([one[: edges[0]].reshape(2, out_rows, block) for one in parts])
    ctx_sums = first[edges[0] : edges[1]].reshape(grp_count, ctx_out, block)
    d_context = jnp.concatenate(list(ctx_sums), axis=1).astype(BF16)
    wo_sums = first[edges[1] :].reshape(grp_count, out_rows, block)
    grad_wo = jnp.concatenate(list(wo_sums), axis=1)
    sent = lax.dynamic_index_in_dim(wq_sums, 1 - core, 1, keepdims=False)
    mine = lax.dynamic_index_in_dim(wq_sums, core, 1, keepdims=False)
    theirs = swap(sent, core_mask)
    pieces = []
    for part in range(high_count):
        pieces.append(jnp.where(core == 0, mine[part], theirs[part]))
        pieces.append(jnp.where(core == 0, theirs[part], mine[part]))
    grad_wq = jnp.concatenate(pieces, axis=1)

    returned = swap(query_partner, core_mask)
    (d_targets,) = call(
        partial(targets_kernel, block),
        [place, query_own, returned, w_query],
        [((query_rows, width), BF16)],
        product,
    )
    return (d_targets, d_context, grad_wq, grad_wo)


def solution(mesh):
    in_specs = (
        P(AXES, None),
        P("seq", None),
        P(),
        P(),
        P(),
        P(),
        P(),
        P(AXES, None),
    )
    out_specs = (P(AXES, None), P(AXES, None), P(AXES, None), P(AXES, None))

    return jax.shard_map(
        on_device, mesh=mesh, in_specs=in_specs, out_specs=out_specs, check_vma=False
    )
```
